256 devices in a mesh: dp: 4 (over x), ep: 64 (over z, y, core).
Axes of the slice: x: 4, y: 4, z: 8, core: 2. Of those that a mesh axis runs over, the one named last changes fastest.
Arguments:
- query_heads: bfloat16 [32768, 2048], P(('dp', 'ep')), parts along dimension 0, may hold values from -6 to 6
- key_heads: bfloat16 [32768, 256], P(('dp', 'ep')), parts along dimension 0, may hold values from -6 to 6
- value_heads: bfloat16 [32768, 256], P(('dp', 'ep')), parts along dimension 0, may hold values from -6 to 6
- out_weight: bfloat16 [2048, 1440], P('ep'), may hold values from -0.75 to 0.75
- norm_gain: float32 [1440], replicated, may hold values from 0.5 to 1.5
- gate_up_weight: bfloat16 [64, 1440, 2880], P('ep'), may hold values from -0.15625 to 0.15625
- down_weight: bfloat16 [64, 1440, 1440], P('ep'), may hold values from -0.15625 to 0.15625
- expert_ids: int32 [32768, 4], P(('dp', 'ep')), parts along dimension 0, may hold values from 0 to 63, as said below
- route_weights: float32 [32768, 4], P(('dp', 'ep')), parts along dimension 0, may hold values from 0.05 to 0.6
Outputs:
- mixed: bfloat16 [32768, 1440], P(('dp', 'ep')), parts along dimension 0
The draws below stay inside these ranges and needn't reach their ends.
There are 4 independent parts, one for each index of `dp`. The reference program is written for one: setup_inputs(seed, part) draws one part's arguments, and reference() takes and returns one part's arrays. A program takes and returns all parts, laid end to end along the dimension named above; an argument that names none is the same for every part. Nothing has to cross between parts.
Inputs may be any that keep to these rules, and one draw needn't show every extreme that they name: `expert_ids`: each row names 4 different experts. In each aligned block of 128 rows (the tokens of one device) one and the same expert is named exactly 16 times in every block, and every other expert fewer than 16 times.
All inputs are finite; a program needn't handle non-finite values.
Results may differ from the reference program's by a relative error of at most 0.0074.
Values may be sent and summed in bfloat16 or wider, within the bound.
No kernel may reach another device: no remote copies, remote signals or barrier semaphores. Data moves between devices by JAX's collectives and lax.ppermute only.
A program may use at most 128 MiB of HBM per device.

```python
import math
import jax
import jax.numpy as jnp
from jax import lax

D = 1440
FF = 1440
QH = 32
KVH = 4
HD = 64
WIN = 128
TOP = 4
TOK_DEV = 128
EXPERTS = 64
TOKENS = 8192
CAP = 16


def shared_heads(key):
    query_key, key_key = jax.random.split(jax.random.fold_in(key, 11), 2)
    query_rows = jax.random.truncated_normal(query_key, -5.0, 5.0, (TOKENS, QH * HD), jnp.float32)
    key_rows = jax.random.truncated_normal(key_key, -5.0, 5.0, (TOKENS, KVH * HD), jnp.float32)
    return (query_rows, key_rows)


def draw_query_heads(key, part):
    return shared_heads(key)[0].astype(jnp.bfloat16)


def draw_key_heads(key, part):
    return shared_heads(key)[1].astype(jnp.bfloat16)


def draw_expert_ids(key, part):
    mean_load = TOK_DEV * TOP // EXPERTS
    hot_key, block_key = jax.random.split(jax.random.fold_in(key, 23))
    hot_expert = jax.random.randint(hot_key, (), 0, EXPERTS)

    def one_block(block_seed):
        perm_key, pair_key, order_key, turn_key = jax.random.split(block_seed, 4)
        expert_order = jax.random.permutation(perm_key, EXPERTS)
        where_hot = jnp.argmax(expert_order == hot_expert)
        first_one = expert_order[0]
        expert_order = expert_order.at[where_hot].set(first_one).at[0].set(hot_expert)
        lift_by = jax.random.randint(pair_key, (EXPERTS // 2,), 0, mean_load)
        lift_by = lift_by.at[0].set(mean_load)
        expert_loads = jnp.zeros((EXPERTS,), jnp.int32)
        expert_loads = expert_loads.at[expert_order[0::2]].set(mean_load + lift_by)
        expert_loads = expert_loads.at[expert_order[1::2]].set(mean_load - lift_by)
        bounds = jnp.cumsum(expert_loads)
        slot_ids = jnp.arange(TOK_DEV * TOP)
        listed = jnp.sum((bounds[None, :] <= slot_ids[:, None]).astype(jnp.int32), axis=1)
        route_grid = listed.reshape(TOP, TOK_DEV).T
        row_order = jax.random.permutation(order_key, TOK_DEV)
        route_grid = route_grid[row_order]
        turn_by = jax.random.randint(turn_key, (TOK_DEV, 1), 0, TOP)
        column_order = (jnp.arange(TOP)[None, :] + turn_by) % TOP
        return jnp.take_along_axis(route_grid, column_order, axis=1)
    block_seeds = jax.random.split(block_key, TOKENS // TOK_DEV)
    return jax.vmap(one_block)(block_seeds).reshape(TOKENS, TOP).astype(jnp.int32)


def block_levels(rng, shape, cuts, smallest, largest):
    def one(axis_at, parts):
        heights = jax.random.uniform(jax.random.fold_in(jax.random.fold_in(rng, 6), axis_at), (parts,), jnp.float32, smallest / len(cuts), largest / len(cuts))
        return jnp.repeat(jnp.exp(heights), shape[axis_at] // parts).reshape((-1,) + (1,) * (len(shape) - axis_at - 1))

    loudness = one(*cuts[0])
    for cut in cuts[1:]:
        loudness = loudness * one(*cut)
    return loudness


def gaussian(rng, dims, deviation, most, shards=(), kind=jnp.bfloat16):
    drawn = deviation * jax.random.normal(rng, dims, jnp.float32)
    if shards:
        drawn = drawn * block_levels(rng, dims, shards, -0.22, 0.18)
    return jnp.clip(drawn, -most, most).astype(kind)


def setup_inputs(seed: int = 0, part: int = 0) -> dict:
    splits = jax.random.split(jax.random.key(seed), 10)
    part_keys = jax.random.split(jax.random.fold_in(splits[9], part), 10)
    return {
        "query_heads": draw_query_heads(jax.random.fold_in(jax.random.fold_in(splits[9], part), 71), part),
        "key_heads": draw_key_heads(jax.random.fold_in(jax.random.fold_in(splits[9], part), 71), part),
        "value_heads": gaussian(part_keys[2], (TOKENS, KVH * HD), 1.0, 6.0, ((0, 64),)),
        "out_weight": gaussian(splits[3], (QH * HD, D), HD ** -0.5, 0.75, ((0, 64),)),
        "norm_gain": jnp.clip(1.0 + 0.1 * jax.random.normal(splits[4], (D,), jnp.float32), 0.5, 1.5),
        "gate_up_weight": gaussian(splits[5], (EXPERTS, D, 2 * FF), D ** -0.5, 0.15625, ((0, 64),)),
        "down_weight": gaussian(splits[6], (EXPERTS, FF, D), FF ** -0.5, 0.15625, ((0, 64),)),
        "expert_ids": draw_expert_ids(jax.random.fold_in(jax.random.fold_in(splits[9], part), 71), part),
        "route_weights": jnp.clip(jnp.exp(math.log(0.6) - 2.4849067 * jax.random.uniform(part_keys[8], (TOKENS, TOP), jnp.float32) ** block_levels(part_keys[8], (TOKENS, TOP), ((0, 64),), -0.2, 0.2)), 0.05, 0.6),
    }


def window_attention(query_block, key_block, value_block, query_first, key_first):
    block_rows = query_block.shape[0]
    key_span = key_block.shape[0]
    kv_heads = key_block.shape[1] // HD
    group_size = query_block.shape[1] // key_block.shape[1]
    query_split = query_block.astype(jnp.float32).reshape(block_rows, kv_heads, group_size, HD)
    key_split = key_block.astype(jnp.float32).reshape(key_span, kv_heads, HD)
    value_split = value_block.astype(jnp.float32).reshape(key_span, kv_heads, HD)
    scores = jnp.einsum('tgjd,sgd->gjts', query_split, key_split) * HD ** (-0.5)
    query_pos = query_first + jnp.arange(block_rows)
    key_pos = key_first + jnp.arange(key_span)
    distance = query_pos[:, None] - key_pos[None, :]
    allowed = (distance >= 0) & (distance < WIN) & (key_pos[None, :] >= 0)
    scores = jnp.where(allowed, scores, -1e+30)
    row_peak = lax.optimization_barrier(jnp.max(scores, axis=-1, keepdims=True))
    exp_scores = jnp.exp(scores - row_peak)
    attn_probs = (exp_scores / lax.optimization_barrier(jnp.sum(exp_scores, axis=-1, keepdims=True))).astype(jnp.bfloat16)
    mixed_heads = jnp.einsum('gjts,sgd->tgjd', attn_probs.astype(jnp.float32), value_split)
    return mixed_heads.reshape(block_rows, -1).astype(jnp.bfloat16)

def expert_apply(token_rows, gate_up_one, down_one):
    projected = jnp.dot(token_rows, gate_up_one, preferred_element_type=jnp.float32)
    hidden_units = down_one.shape[0]
    gate_part = projected[:, :hidden_units]
    up_part = projected[:, hidden_units:]
    activated = ((up_part + 1.0) * gate_part * jax.nn.sigmoid(1.702 * gate_part)).astype(jnp.bfloat16)
    return jnp.dot(activated, down_one, preferred_element_type=jnp.float32).astype(jnp.bfloat16)

def reference(query_heads, key_heads, value_heads, out_weight, norm_gain, gate_up_weight, down_weight, expert_ids, route_weights):
    block_rows = min(TOK_DEV, 512)
    pad_keys = jnp.concatenate([jnp.zeros((WIN, key_heads.shape[1]), jnp.bfloat16), key_heads], 0)
    pad_values = jnp.concatenate([jnp.zeros((WIN, value_heads.shape[1]), jnp.bfloat16), value_heads], 0)

    def one_block(block_index):
        start_row = block_index * block_rows
        query_block = lax.dynamic_slice_in_dim(query_heads, start_row, block_rows, 0)
        key_block = lax.dynamic_slice_in_dim(pad_keys, start_row, block_rows + WIN, 0)
        value_block = lax.dynamic_slice_in_dim(pad_values, start_row, block_rows + WIN, 0)
        return window_attention(query_block, key_block, value_block, start_row, start_row - WIN)
    context = lax.map(one_block, jnp.arange(TOKENS // block_rows, dtype=jnp.int32)).reshape(TOKENS, -1)
    hidden = jnp.dot(context, out_weight, preferred_element_type=jnp.float32).astype(jnp.bfloat16)
    hidden_f = lax.optimization_barrier(hidden).astype(jnp.float32)
    scale_rms = lax.rsqrt(lax.optimization_barrier(jnp.mean(hidden_f * hidden_f, axis=-1, keepdims=True)) + 1e-05)
    normed = (hidden_f * scale_rms * norm_gain).astype(jnp.bfloat16)
    flat_ids = expert_ids.reshape(-1).astype(jnp.int32)
    route_total = flat_ids.shape[0]
    onehot = (flat_ids[:, None] == jnp.arange(EXPERTS, dtype=jnp.int32)[None, :]).astype(jnp.int32)
    slot_rank = lax.optimization_barrier(jnp.sum((jnp.cumsum(onehot, axis=0) - onehot) * onehot, axis=1)).astype(jnp.int32)
    slot_table = jnp.full((EXPERTS, EXPERTS * CAP), route_total, jnp.int32)
    slot_table = slot_table.at[flat_ids, slot_rank].set(jnp.arange(route_total, dtype=jnp.int32))
    normed_pad = jnp.concatenate([normed, jnp.zeros((1, D), jnp.bfloat16)], 0)

    def one_expert(operands):
        gate_up_one, down_one, slot_row = operands
        return expert_apply(normed_pad[slot_row // TOP], gate_up_one, down_one)
    expert_out = lax.map(one_expert, (gate_up_weight, down_weight, slot_table))
    routed = expert_out[flat_ids, slot_rank].astype(jnp.float32).reshape(TOKENS, TOP, D)
    moe_out = lax.optimization_barrier(jnp.sum(routed * route_weights[:, :, None], axis=1))
    return (hidden_f + moe_out).astype(jnp.bfloat16)
```

```python
import jax
import jax.numpy as jnp
from jax import lax
from jax.sharding import PartitionSpec as P

HD = 64
WIN = 128
NZ, NY, NC = 8, 4, 2
CAP = 16
HALF = 768
PLANE = NY * NC * CAP
GROUPS = ((0, 1, -1), (2, -2), (3, -3, 4))
BF16 = jnp.bfloat16
F32 = jnp.float32


def index_of(z, y, c):
    return ((z % NZ) * NY + y % NY) * NC + c


def moved(block, dz=0, dy=0, flip=False):
    route = [
        (index_of(z, y, c), index_of(z + dz, y + dy, 1 - c if flip else c))
        for z in range(NZ)
        for y in range(NY)
        for c in range(NC)
    ]
    return lax.ppermute(block, "ep", route)


def from_behind(block, distance):
    devices = range(NZ * NY * NC)
    route = [(i - distance, i) for i in devices if i - distance in devices]
    return lax.ppermute(block, "ep", route)


def window_attention(query_block, key_block, value_block, query_first, key_first):
    block_rows = query_block.shape[0]
    key_span = key_block.shape[0]
    kv_heads = key_block.shape[1] // HD
    group_size = query_block.shape[1] // key_block.shape[1]
    query_split = query_block.reshape(block_rows, kv_heads, group_size, HD)
    key_split = key_block.reshape(key_span, kv_heads, HD)
    value_split = value_block.reshape(key_span, kv_heads, HD)
    scores = jnp.einsum(
        "tgjd,sgd->gjts", query_split, key_split, preferred_element_type=F32
    ) * HD ** (-0.5)
    query_pos = query_first + jnp.arange(block_rows)
    key_pos = key_first + jnp.arange(key_span)
    distance = query_pos[:, None] - key_pos[None, :]
    allowed = (distance >= 0) & (distance < WIN) & (key_pos[None, :] >= 0)
    scores = jnp.where(allowed, scores, -1e30)
    row_peak = jnp.max(scores, axis=-1, keepdims=True)
    exp_scores = jnp.exp(scores - row_peak)
    attn_probs = (exp_scores / jnp.sum(exp_scores, axis=-1, keepdims=True)).astype(BF16)
    mixed_heads = jnp.einsum(
        "gjts,sgd->tgjd", attn_probs, value_split, preferred_element_type=F32
    )
    return mixed_heads.reshape(block_rows, -1).astype(BF16)


def expert_apply(token_rows, gate_up_one, down_one):
    projected = jnp.dot(token_rows, gate_up_one, preferred_element_type=F32)
    hidden_units = down_one.shape[0]
    gate_part = projected[:, :hidden_units]
    up_part = projected[:, hidden_units:]
    activated = ((up_part + 1.0) * gate_part * jax.nn.sigmoid(1.702 * gate_part)).astype(BF16)
    return jnp.dot(activated, down_one, preferred_element_type=F32).astype(BF16)


def ring(block):
    rows = block.shape[0] // 2
    got = {0: block}
    up, down = block, block
    for step in (1, 2, 3):
        up, down = moved(up, dz=1), moved(down, dz=-1)
        got[-step], got[step] = up, down
    low, high = moved(up[:rows], dz=1), moved(down[rows:], dz=-1)
    got[4] = jnp.concatenate([low, high], 0)
    return got


def projection(context, out_weight, z, y, c):
    width = out_weight.shape[1]
    halves = jnp.pad(out_weight, ((0, 0), (0, 2 * HALF - width)))
    left, right = halves[:, :HALF], halves[:, HALF:]
    first = c == 0
    kept = jnp.where(first, left, right)
    swapped = moved(jnp.where(first, right, left), flip=True)
    chip = jnp.where(
        first, jnp.concatenate([kept, swapped], 0), jnp.concatenate([swapped, kept], 0)
    )
    around = [chip, moved(chip, dy=-1), moved(chip, dy=2), moved(chip, dy=1)]
    plane = lax.dynamic_slice_in_dim(jnp.stack(around + around), (NY - y) % NY, NY, 0)
    plane = plane.reshape(-1, HALF)
    both = jnp.concatenate([context, moved(context, flip=True)], 0)
    depth = plane.shape[0]
    both = both.reshape(-1, NZ, depth).transpose(1, 0, 2)
    total = 0.0
    for d, part in ring(plane).items():
        columns = lax.dynamic_index_in_dim(both, (z + d) % NZ, 0, keepdims=False)
        total += jnp.dot(columns, part, preferred_element_type=F32)
    total = total.astype(BF16)
    rows = context.shape[0]
    mine, other = total[:rows], moved(total[rows:], flip=True)
    whole = jnp.where(
        first, jnp.concatenate([mine, other], 1), jnp.concatenate([other, mine], 1)
    )
    return whole[:, :width]


def slots_of(expert_ids):
    rows = expert_ids.shape[0]
    experts = jnp.arange(NZ * NY * NC, dtype=jnp.int32)
    named = expert_ids[:, :, None] == experts
    marks = jnp.sum(named.astype(F32), axis=1).astype(BF16)
    steps = jnp.arange(rows)
    earlier = (steps[:, None] > steps[None, :]).astype(BF16)
    counts = jnp.dot(earlier, marks, preferred_element_type=F32)
    rank = jnp.sum(jnp.where(named, counts[:, None, :], 0.0), axis=2)
    return expert_ids.astype(F32) * CAP + rank


def send_out(parts, size):
    piece = lambda a, i: a[i * size : (i + 1) * size]
    plus = moved(parts[2 * size : 5 * size], dy=1)
    minus = moved(parts[5 * size :], dy=-1)
    far_same = moved(piece(plus, 2), dy=1)
    far_flip = moved(piece(minus, 0), dy=-1, flip=True)
    swapped = moved(
        jnp.concatenate([piece(parts, 1), piece(plus, 1), piece(minus, 2)], 0), flip=True
    )
    return jnp.concatenate(
        [piece(parts, 0), piece(plus, 0), piece(minus, 1), far_same, far_flip, swapped], 0
    )


def bring_back(rows, size):
    piece = lambda a, i: a[i * size : (i + 1) * size]
    swapped = moved(rows[5 * size :], flip=True)
    far_same = moved(piece(rows, 3), dy=-1)
    far_flip = moved(piece(rows, 4), dy=1, flip=True)
    minus = moved(jnp.concatenate([piece(rows, 1), piece(swapped, 1), far_same], 0), dy=-1)
    plus = moved(jnp.concatenate([far_flip, piece(rows, 2), piece(swapped, 2)], 0), dy=1)
    return jnp.concatenate([piece(rows, 0), piece(swapped, 0), minus, plus], 0)


def shards(
    query_heads,
    key_heads,
    value_heads,
    out_weight,
    norm_gain,
    gate_up_weight,
    down_weight,
    expert_ids,
    route_weights,
):
    tok_rows = query_heads.shape[0]
    device_index = lax.axis_index("ep")
    z, y, c = device_index // (NY * NC), device_index // NC % NY, device_index % NC
    first_pos = device_index * tok_rows
    prev_keys, prev_values = from_behind((key_heads, value_heads), 1)
    keys_all = jnp.concatenate([prev_keys, key_heads], 0)
    values_all = jnp.concatenate([prev_values, value_heads], 0)
    context = window_attention(query_heads, keys_all, values_all, first_pos, first_pos - WIN)
    hidden = projection(context, out_weight, z, y, c)

    plans = jnp.concatenate([slots_of(expert_ids).T, route_weights.T], 0)
    same_line = [
        [index_of(zz, yy, cc) for zz in range(NZ)] for yy in range(NY) for cc in range(NC)
    ]
    plans = lax.all_gather(plans, "ep", axis=0, axis_index_groups=same_line)
    route_count = expert_ids.shape[1]

    hidden_f = lax.optimization_barrier(hidden).astype(F32)
    scale_rms = lax.rsqrt(jnp.mean(hidden_f * hidden_f, axis=-1, keepdims=True) + 1e-05)
    normed = (hidden_f * scale_rms * norm_gain).astype(BF16)

    blocks = ring(normed)
    partial = {}
    for group in GROUPS:
        size = CAP * len(group)
        slots = jnp.arange(NY * NC * size, dtype=jnp.int32)[:, None]
        picked, weights = 0.0, []
        for at, d in enumerate(group):
            plan = lax.dynamic_index_in_dim(plans, (z + d) % NZ, 0, keepdims=False)
            place = plan[:route_count].astype(jnp.int32) - z * PLANE
            here = (place >= 0) & (place < PLANE)
            to_y, to_c = place // (NC * CAP), place // CAP % NC
            way = (to_y - y) % NY * NC + (to_c ^ c)
            row = jnp.where(here, way * size + at * CAP + place % CAP, -1)
            hits = row[:, None, :] == slots[None]
            pick = jnp.any(hits, axis=0).astype(BF16)
            picked += jnp.dot(pick, blocks[d], preferred_element_type=F32)
            weights.append(
                jnp.sum(jnp.where(hits, plan[route_count:][:, None, :], 0.0), axis=0)
            )
        rows = send_out(picked.astype(BF16), size)
        made = expert_apply(rows, gate_up_weight[0], down_weight[0])
        made = bring_back(made, size)
        for weight, d in zip(weights, group):
            coarse = lax.reduce_precision(weight, 8, 7)
            fine = (weight - coarse).astype(BF16)
            total = 0.0
            for term in (coarse.astype(BF16), fine):
                total += lax.dot_general(
                    term, made, (((0,), (0,)), ((), ())), preferred_element_type=F32
                )
            partial[d] = total
    rows = tok_rows // 2
    up = moved(partial[4][rows:].astype(BF16), dz=1).astype(F32)
    down = moved(partial[4][:rows].astype(BF16), dz=-1).astype(F32)
    up = jnp.concatenate([partial[3][:rows], partial[3][rows:] + up], 0)
    down = jnp.concatenate([partial[-3][:rows] + down, partial[-3][rows:]], 0)
    for step in (2, 1, 0):
        up = moved(up.astype(BF16), dz=1).astype(F32)
        down = moved(down.astype(BF16), dz=-1).astype(F32)
        if step:
            up, down = up + partial[step], down + partial[-step]
    return (hidden_f + (partial[0] + up + down)).astype(BF16)


def solution(mesh):
    placed = (
        P(("dp", "ep"), None),
        P(("dp", "ep"), None),
        P(("dp", "ep"), None),
        P("ep", None),
        P(),
        P("ep", None, None),
        P("ep", None, None),
        P(("dp", "ep"), None),
        P(("dp", "ep"), None),
    )
    return jax.shard_map(
        shards, mesh=mesh, in_specs=placed, out_specs=P(("dp", "ep"), None), check_vma=False
    )
```

```python
import jax
import jax.numpy as jnp
from jax import lax
from jax.sharding import PartitionSpec as P

HD = 64
WIN = 128
NX, NZ, NY, NC = 4, 8, 4, 2
CAP = 16
QUARTER = 384
BF16 = jnp.bfloat16
F32 = jnp.float32


def index_of(z, y, c):
    return ((z % NZ) * NY + y % NY) * NC + c


def moved(block, dz=0, dy=0, flip=False):
    route = [
        (index_of(z, y, c), index_of(z + dz, y + dy, 1 - c if flip else c))
        for z in range(NZ)
        for y in range(NY)
        for c in range(NC)
    ]
    return lax.ppermute(block, "ep", route)


def from_behind(block, distance):
    devices = range(NZ * NY * NC)
    route = [(i - distance, i) for i in devices if i - distance in devices]
    return lax.ppermute(block, "ep", route)


def window_attention(query_block, key_block, value_block, query_first, key_first):
    block_rows = query_block.shape[0]
    key_span = key_block.shape[0]
    kv_heads = key_block.shape[1] // HD
    group_size = query_block.shape[1] // key_block.shape[1]
    query_split = query_block.reshape(block_rows, kv_heads, group_size, HD)
    key_split = key_block.reshape(key_span, kv_heads, HD)
    value_split = value_block.reshape(key_span, kv_heads, HD)
    scores = jnp.einsum(
        "tgjd,sgd->gjts", query_split, key_split, preferred_element_type=F32
    ) * HD ** (-0.5)
    query_pos = query_first + jnp.arange(block_rows)
    key_pos = key_first + jnp.arange(key_span)
    distance = query_pos[:, None] - key_pos[None, :]
    allowed = (distance >= 0) & (distance < WIN) & (key_pos[None, :] >= 0)
    scores = jnp.where(allowed, scores, -1e30)
    row_peak = jnp.max(scores, axis=-1, keepdims=True)
    exp_scores = jnp.exp(scores - row_peak)
    attn_probs = (exp_scores / jnp.sum(exp_scores, axis=-1, keepdims=True)).astype(BF16)
    mixed_heads = jnp.einsum(
        "gjts,sgd->tgjd", attn_probs, value_split, preferred_element_type=F32
    )
    return mixed_heads.reshape(block_rows, -1).astype(BF16)


def expert_apply(token_rows, gate_up_one, down_one):
    projected = jnp.dot(token_rows, gate_up_one, preferred_element_type=F32)
    hidden_units = down_one.shape[0]
    gate_part = projected[:, :hidden_units]
    up_part = projected[:, hidden_units:]
    activated = ((up_part + 1.0) * gate_part * jax.nn.sigmoid(1.702 * gate_part)).astype(BF16)
    return jnp.dot(activated, down_one, preferred_element_type=F32).astype(BF16)


def ring(block):
    rows = block.shape[0] // 2
    got = {0: block}
    up, down = block, block
    for step in (1, 2, 3):
        up, down = moved(up, dz=1), moved(down, dz=-1)
        got[-step], got[step] = up, down
    low, high = moved(up[:rows], dz=1), moved(down[rows:], dz=-1)
    got[4] = jnp.concatenate([low, high], 0)
    return got


def moved_x(block, dx):
    return lax.ppermute(block, "dp", [(x, (x + dx) % NX) for x in range(NX)])


def in_order(pieces, first, count):
    return lax.dynamic_slice_in_dim(jnp.stack(pieces + pieces), (count - first) % count, count, 0)


def projection(context, out_weight, x, z, y, c):
    depth, width = out_weight.shape
    padded = jnp.pad(out_weight, ((0, 0), (0, NX * QUARTER - width)))
    kept = lax.dynamic_slice_in_dim(padded, x * QUARTER, QUARTER, 1)
    swapped = moved(kept, flip=True)
    chip = in_order([kept, swapped], c, NC).reshape(-1, QUARTER)
    around = [chip, moved(chip, dy=-1), moved(chip, dy=2), moved(chip, dy=1)]
    plane = in_order(around, y, NY).reshape(-1, QUARTER)
    parts = ring(plane)

    rows = context.shape[0]
    up, down = moved_x(context, 1), moved_x(context, -1)
    low, high = moved_x(up[: rows // 2], 1), moved_x(down[rows // 2 :], -1)
    all_rows = jnp.concatenate([context, down, low, high, up], 0)
    all_rows = all_rows.reshape(NX * rows, NZ, -1).transpose(1, 0, 2)
    total = 0.0
    for d, part in parts.items():
        columns = lax.dynamic_index_in_dim(all_rows, (z + d) % NZ, 0, keepdims=False)
        total += jnp.dot(columns, part, preferred_element_type=F32)
    total = total.astype(BF16).reshape(NX, rows, QUARTER)
    quarters = [
        total[0],
        moved_x(total[3], -1),
        moved_x(total[2], 2),
        moved_x(total[1], 1),
    ]
    quarters = in_order(quarters, x, NX)
    return jnp.concatenate([quarters[i] for i in range(NX)], 1)[:, :width]


def slots_of(expert_ids):
    rows = expert_ids.shape[0]
    experts = jnp.arange(NZ * NY * NC, dtype=jnp.int32)
    named = expert_ids[:, :, None] == experts
    marks = jnp.sum(named.astype(F32), axis=1).astype(BF16)
    steps = jnp.arange(rows)
    earlier = (steps[:, None] > steps[None, :]).astype(BF16)
    counts = jnp.dot(earlier, marks, preferred_element_type=F32)
    rank = jnp.sum(jnp.where(named, counts[:, None, :], 0.0), axis=2)
    return expert_ids.astype(F32) * CAP + rank


def shards(
    query_heads,
    key_heads,
    value_heads,
    out_weight,
    norm_gain,
    gate_up_weight,
    down_weight,
    expert_ids,
    route_weights,
):
    tok_rows = query_heads.shape[0]
    device_index = lax.axis_index("ep")
    z, y, c = device_index // (NY * NC), device_index // NC % NY, device_index % NC
    first_pos = device_index * tok_rows
    prev_keys, prev_values = from_behind((key_heads, value_heads), 1)
    keys_all = jnp.concatenate([prev_keys, key_heads], 0)
    values_all = jnp.concatenate([prev_values, value_heads], 0)
    context = window_attention(query_heads, keys_all, values_all, first_pos, first_pos - WIN)
    hidden = projection(context, out_weight, lax.axis_index("dp"), z, y, c)

    places = NZ * NY * NC * CAP
    hits = slots_of(expert_ids).T[:, None, :] == jnp.arange(places)[None, :, None]
    pick = jnp.any(hits, axis=0).astype(BF16)
    weight = jnp.sum(jnp.where(hits, route_weights.T[:, None, :], 0.0), axis=0)
    coarse = lax.reduce_precision(weight, 8, 7)
    fine = (weight - coarse).astype(BF16)
    coarse = coarse.astype(BF16)

    hidden_f = lax.optimization_barrier(hidden).astype(F32)
    scale_rms = lax.rsqrt(jnp.mean(hidden_f * hidden_f, axis=-1, keepdims=True) + 1e-05)
    normed = (hidden_f * scale_rms * norm_gain).astype(BF16)
    sent = jnp.dot(pick, normed, preferred_element_type=F32).astype(BF16)

    def exchange(rows):
        rows = rows.reshape(NZ * NY * NC, CAP, -1)
        rows = lax.all_to_all(rows, "ep", split_axis=0, concat_axis=0, tiled=True)
        return rows.reshape(places, -1)

    made = exchange(expert_apply(exchange(sent), gate_up_weight[0], down_weight[0]))
    moe_out = 0.0
    for term in (coarse, fine):
        moe_out += lax.dot_general(
            term, made, (((0,), (0,)), ((), ())), preferred_element_type=F32
        )
    return (hidden_f + moe_out).astype(BF16)


def solution(mesh):
    placed = (
        P(("dp", "ep"), None),
        P(("dp", "ep"), None),
        P(("dp", "ep"), None),
        P("ep", None),
        P(),
        P("ep", None, None),
        P("ep", None, None),
        P(("dp", "ep"), None),
        P(("dp", "ep"), None),
    )
    return jax.shard_map(
        shards, mesh=mesh, in_specs=placed, out_specs=P(("dp", "ep"), None), check_vma=False
    )
```

```python
import jax
import jax.numpy as jnp
from jax import lax
from jax.experimental import pallas as pl
from jax.experimental.pallas import tpu as pltpu
from jax.sharding import PartitionSpec as P

HD = 64
WIN = 128
NX, NZ, NY, NC = 4, 8, 4, 2
CAP = 16
QUARTER = 384
SLOTS = NY * NC * CAP
GROUPS = ((0, 1, -1, 2, -2), (3, -3, 4))
WAYS = tuple((dy, flip) for dy in range(NY) for flip in range(NC))
TOP = 4
BF16 = jnp.bfloat16
F32 = jnp.float32


def index_of(z, y, c):
    return ((z % NZ) * NY + y % NY) * NC + c


def moved(block, dz=0, dy=0, flip=False):
    if not (dz or dy or flip):
        return block
    route = [
        (index_of(z, y, c), index_of(z + dz, y + dy, 1 - c if flip else c))
        for z in range(NZ)
        for y in range(NY)
        for c in range(NC)
    ]
    return lax.ppermute(block, "ep", route)


def from_behind(block, distance):
    devices = range(NZ * NY * NC)
    route = [(i - distance, i) for i in devices if i - distance in devices]
    return lax.ppermute(block, "ep", route)


def window_attention(query_block, key_block, value_block, query_first, key_first):
    block_rows = query_block.shape[0]
    key_span = key_block.shape[0]
    kv_heads = key_block.shape[1] // HD
    group_size = query_block.shape[1] // key_block.shape[1]
    query_split = query_block.reshape(block_rows, kv_heads, group_size, HD)
    key_split = key_block.reshape(key_span, kv_heads, HD)
    value_split = value_block.reshape(key_span, kv_heads, HD)
    scores = jnp.einsum(
        "tgjd,sgd->gjts", query_split, key_split, preferred_element_type=F32
    ) * HD ** (-0.5)
    query_pos = query_first + jnp.arange(block_rows)
    key_pos = key_first + jnp.arange(key_span)
    distance = query_pos[:, None] - key_pos[None, :]
    allowed = (distance >= 0) & (distance < WIN) & (key_pos[None, :] >= 0)
    scores = jnp.where(allowed, scores, -1e30)
    row_peak = jnp.max(scores, axis=-1, keepdims=True)
    exp_scores = jnp.exp(scores - row_peak)
    attn_probs = (exp_scores / jnp.sum(exp_scores, axis=-1, keepdims=True)).astype(BF16)
    mixed_heads = jnp.einsum(
        "gjts,sgd->tgjd", attn_probs, value_split, preferred_element_type=F32
    )
    return mixed_heads.reshape(block_rows, -1).astype(BF16)


def ring(block):
    rows = block.shape[0] // 2
    got = {0: block}
    up, down = block, block
    for step in (1, 2, 3):
        up, down = moved(up, dz=1), moved(down, dz=-1)
        got[-step], got[step] = up, down
    low, high = moved(up[:rows], dz=1), moved(down[rows:], dz=-1)
    got[4] = (low, high)
    return got


def moved_x(block, dx):
    return lax.ppermute(block, "dp", [(x, (x + dx) % NX) for x in range(NX)])


def in_order(pieces, first, count):
    return lax.dynamic_slice_in_dim(jnp.stack(pieces + pieces), (count - first) % count, count, 0)


def projection(context, out_weight, plan, x, z, y, c):
    depth, width = out_weight.shape
    padded = jnp.pad(out_weight, ((0, 0), (0, NX * QUARTER - width)))
    kept = lax.dynamic_slice_in_dim(padded, x * QUARTER, QUARTER, 1)
    swapped = moved(kept, flip=True)
    chip = in_order([kept, swapped], c, NC).reshape(-1, QUARTER)
    around = [chip, moved(chip, dy=-1), moved(chip, dy=2), moved(chip, dy=1)]
    plane = in_order(around, y, NY).reshape(-1, QUARTER)
    taken = plane.shape[0]
    parts = ring(jnp.concatenate([plane, plan], 0))
    parts[4] = jnp.concatenate(parts[4], 0)
    plans = {d: part[taken:] for d, part in parts.items()}

    rows = context.shape[0]
    up, down = moved_x(context, 1), moved_x(context, -1)
    low, high = moved_x(up[: rows // 2], 1), moved_x(down[rows // 2 :], -1)
    all_rows = jnp.concatenate([context, down, low, high, up], 0)
    all_rows = all_rows.reshape(NX * rows, NZ, -1).transpose(1, 0, 2)
    total = 0.0
    for d, part in parts.items():
        columns = lax.dynamic_index_in_dim(all_rows, (z + d) % NZ, 0, keepdims=False)
        total += jnp.dot(columns, part[:taken], preferred_element_type=F32)
    total = total.astype(BF16).reshape(NX, rows, QUARTER)
    quarters = [
        total[0],
        moved_x(total[3], -1),
        moved_x(total[2], 2),
        moved_x(total[1], 1),
    ]
    quarters = in_order(quarters, x, NX)
    return jnp.concatenate([quarters[i] for i in range(NX)], 1)[:, :width], plans


def ranks_of(expert_ids):
    rows = expert_ids.shape[0]
    experts = jnp.arange(NZ * NY * NC, dtype=jnp.int32)
    named = expert_ids[:, :, None] == experts
    marks = jnp.sum(named.astype(F32), axis=1).astype(BF16)
    steps = jnp.arange(rows)
    earlier = (steps[:, None] > steps[None, :]).astype(BF16)
    counts = jnp.dot(earlier, marks, preferred_element_type=F32)
    return jnp.sum(jnp.where(named, counts[:, None, :], 0.0), axis=2)


def call(body, outs, args, scratch=(), flops=0, limit=40):
    moved_bytes = sum(a.size * a.dtype.itemsize for a in (*args, *outs))
    return pl.pallas_call(
        body,
        out_shape=tuple(outs),
        in_specs=[pl.BlockSpec(memory_space=pltpu.VMEM)] * len(args),
        out_specs=tuple(pl.BlockSpec(memory_space=pltpu.VMEM) for _ in outs),
        scratch_shapes=list(scratch),
        compiler_params=pltpu.CompilerParams(vmem_limit_bytes=limit << 20),
        cost_estimate=pl.CostEstimate(
            flops=flops, bytes_accessed=moved_bytes, transcendentals=0
        ),
    )(*args)


def pick_rows(spots, blocks):
    pieces = [b if isinstance(b, tuple) else (b,) for b in blocks]
    flat = [piece for b in pieces for piece in b]
    count, (rows, width) = len(blocks), blocks[0].shape

    def body(spots_ref, *refs):
        ins, outs, whole = refs[: len(flat)], refs[len(flat) : -1], refs[-1]
        slot = lax.broadcasted_iota(jnp.int32, (SLOTS, rows), 0)
        at = 0
        for b in range(count):
            if len(pieces[b]) > 1:
                first = 0
                for piece in pieces[b]:
                    whole[first : first + piece.shape[0], :] = ins[at][...]
                    first, at = first + piece.shape[0], at + 1
                block = whole[...]
            else:
                block, at = ins[at][...], at + 1
            pick = jnp.zeros((SLOTS, rows), F32)
            for r in range(TOP):
                pick += jnp.where(spots_ref[b, r : r + 1, :] == slot, 1.0, 0.0)
            found = jnp.dot(pick.astype(BF16), block, preferred_element_type=F32).astype(BF16)
            for i in range(len(WAYS)):
                outs[i][b * CAP : (b + 1) * CAP, :] = found[i * CAP : (i + 1) * CAP]

    outs = [jax.ShapeDtypeStruct((count * CAP, width), BF16)] * len(WAYS)
    flops = 2 * count * SLOTS * rows * width
    return call(body, outs, [spots, *flat], [pltpu.VMEM((rows, width), BF16)], flops)


def run_expert(parts, gate_up, down):
    rows, width = parts[0].shape
    total, units = rows * len(parts), down.shape[0]
    wide = 512

    def body(gate_up_ref, down_ref, *refs):
        ins, outs = refs[: len(parts)], refs[len(parts) : -2]
        taken, projected = refs[-2:]
        for i, part in enumerate(ins):
            taken[i * rows : (i + 1) * rows, :] = part[...]
        for first in range(0, 2 * units, wide):
            last = min(first + wide, 2 * units)
            projected[:, first:last] = jnp.dot(
                taken[...], gate_up_ref[:, first:last], preferred_element_type=F32
            )
        for first in range(0, total, rows):
            gate = projected[first : first + rows, :units]
            up = projected[first : first + rows, units:]
            active = (up + 1.0) * gate * jax.nn.sigmoid(1.702 * gate)
            taken[first : first + rows, :] = active.astype(BF16)
        for first in range(0, width, wide):
            last = min(first + wide, width)
            made = jnp.dot(taken[...], down_ref[:, first:last], preferred_element_type=F32)
            made = made.astype(BF16)
            for i, out in enumerate(outs):
                out[:, first:last] = made[i * rows : (i + 1) * rows]

    outs = [jax.ShapeDtypeStruct((rows, width), BF16)] * len(parts)
    scratch = [pltpu.VMEM((total, width), BF16), pltpu.VMEM((total, 2 * units), F32)]
    flops = 6 * total * width * units
    return call(body, outs, [gate_up, down, *parts], scratch, flops)


def combine(spots, shares, parts, count):
    width = parts[0].shape[1]
    rows = spots.shape[2]

    def body(spots_ref, shares_ref, *refs):
        ins, outs, whole = refs[: len(parts)], refs[len(parts) : -1], refs[-1]
        slot = lax.broadcasted_iota(jnp.int32, (SLOTS, rows), 0)
        for b in range(count):
            for i, part in enumerate(ins):
                whole[i * CAP : (i + 1) * CAP, :] = part[b * CAP : (b + 1) * CAP, :]
            sums = 0.0
            for fine in range(2):
                share = jnp.zeros((SLOTS, rows), F32)
                for r in range(TOP):
                    here = spots_ref[b, r : r + 1, :] == slot
                    at = fine * TOP + r
                    share += jnp.where(here, shares_ref[b, at : at + 1, :], 0.0)
                sums += jnp.dot(share.T.astype(BF16), whole[...], preferred_element_type=F32)
            outs[b][...] = sums

    outs = [jax.ShapeDtypeStruct((rows, width), F32)] * count
    flops = 4 * count * SLOTS * rows * width
    return call(body, outs, [spots, shares, *parts], [pltpu.VMEM((SLOTS, width), BF16)], flops)


def shards(
    query_heads,
    key_heads,
    value_heads,
    out_weight,
    norm_gain,
    gate_up_weight,
    down_weight,
    expert_ids,
    route_weights,
):
    tok_rows = query_heads.shape[0]
    device_index = lax.axis_index("ep")
    z, y, c = device_index // (NY * NC), device_index // NC % NY, device_index % NC
    first_pos = device_index * tok_rows
    prev_keys, prev_values = from_behind((key_heads, value_heads), 1)
    keys_all = jnp.concatenate([prev_keys, key_heads], 0)
    values_all = jnp.concatenate([prev_values, value_heads], 0)
    context = window_attention(query_heads, keys_all, values_all, first_pos, first_pos - WIN)
    coarse = lax.reduce_precision(route_weights, 8, 7)
    fine = lax.reduce_precision(route_weights - coarse, 8, 7)
    plan = [jnp.concatenate([a.T, b.T], 0) for a, b in (
        (expert_ids.astype(F32), ranks_of(expert_ids)), (coarse, fine))]
    plan = jnp.concatenate(plan + [jnp.zeros_like(plan[0])], 1).astype(BF16)
    plan = jnp.concatenate([plan, jnp.zeros_like(plan)], 0)
    hidden, plans = projection(context, out_weight, plan, lax.axis_index("dp"), z, y, c)

    near = [d for group in GROUPS for d in group]
    plans = jnp.stack([plans[d] for d in near]).astype(F32)
    shares = plans[:, : 2 * TOP, tok_rows : 2 * tok_rows]
    expert = plans[:, :TOP, :tok_rows].astype(jnp.int32) - z * (NY * NC)
    rank = plans[:, TOP : 2 * TOP, :tok_rows].astype(jnp.int32)
    way = (expert // NC - y) % NY * NC + (expert % NC ^ c)
    here = (expert >= 0) & (expert < NY * NC)
    spots = jnp.where(here, way * CAP + rank, -1)

    hidden_f = lax.optimization_barrier(hidden).astype(F32)
    scale_rms = lax.rsqrt(jnp.mean(hidden_f * hidden_f, axis=-1, keepdims=True) + 1e-05)
    normed = (hidden_f * scale_rms * norm_gain).astype(BF16)

    blocks = ring(normed)
    partial, at = {}, 0
    for group in GROUPS:
        there = slice(at, at + len(group))
        at += len(group)
        rows = pick_rows(spots[there], [blocks[d] for d in group])
        rows = [moved(a, dy=dy, flip=flip) for a, (dy, flip) in zip(rows, WAYS)]
        made = run_expert(rows, gate_up_weight[0], down_weight[0])
        made = [moved(a, dy=-dy, flip=flip) for a, (dy, flip) in zip(made, WAYS)]
        sums = combine(spots[there], shares[there], made, len(group))
        partial.update(zip(group, sums))
    rows = tok_rows // 2
    up = moved(partial[4][rows:].astype(BF16), dz=1).astype(F32)
    down = moved(partial[4][:rows].astype(BF16), dz=-1).astype(F32)
    up = partial[3] + jnp.pad(up, ((rows, 0), (0, 0)))
    down = partial[-3] + jnp.pad(down, ((0, rows), (0, 0)))
    for step in (2, 1, 0):
        up = moved(up.astype(BF16), dz=1).astype(F32)
        down = moved(down.astype(BF16), dz=-1).astype(F32)
        if step:
            up, down = up + partial[step], down + partial[-step]
    return (hidden_f + (partial[0] + up + down)).astype(BF16)


def solution(mesh):
    placed = (
        P(("dp", "ep"), None),
        P(("dp", "ep"), None),
        P(("dp", "ep"), None),
        P("ep", None),
        P(),
        P("ep", None, None),
        P("ep", None, None),
        P(("dp", "ep"), None),
        P(("dp", "ep"), None),
    )
    return jax.shard_map(
        shards, mesh=mesh, in_specs=placed, out_specs=P(("dp", "ep"), None), check_vma=False
    )
```

```python
import jax
import jax.numpy as jnp
from jax import lax
from jax.experimental import pallas as pl
from jax.experimental.pallas import tpu as pltpu
from jax.sharding import PartitionSpec as P

HD = 64
WIN = 128
NX, NZ, NY, NC = 4, 8, 4, 2
CAP = 16
QUARTER = 384
SLOTS = NY * NC * CAP
GROUPS = ((0, 1, -1, 2, -2), (3, -3, 4))
WAYS = tuple((dy, flip) for dy in range(NY) for flip in range(NC))
TOP = 4
EARLY, LATE = (0, 2, 6, 4), (3, 7, 5, 1)
BF16 = jnp.bfloat16
F32 = jnp.float32


def tied(values):
    return lax.optimization_barrier(values)


def index_of(z, y, c):
    return ((z % NZ) * NY + y % NY) * NC + c


def moved(block, dz=0, dy=0, flip=False):
    if not (dz or dy or flip):
        return block
    route = [
        (index_of(z, y, c), index_of(z + dz, y + dy, 1 - c if flip else c))
        for z in range(NZ)
        for y in range(NY)
        for c in range(NC)
    ]
    return lax.ppermute(block, "ep", route)


def from_behind(block, distance):
    devices = range(NZ * NY * NC)
    route = [(i - distance, i) for i in devices if i - distance in devices]
    return lax.ppermute(block, "ep", route)


def window_attention(query_block, key_block, value_block, query_first, key_first):
    block_rows = query_block.shape[0]
    key_span = key_block.shape[0]
    kv_heads = key_block.shape[1] // HD
    group_size = query_block.shape[1] // key_block.shape[1]
    query_split = query_block.reshape(block_rows, kv_heads, group_size, HD)
    key_split = key_block.reshape(key_span, kv_heads, HD)
    value_split = value_block.reshape(key_span, kv_heads, HD)
    scores = jnp.einsum(
        "tgjd,sgd->gjts", query_split, key_split, preferred_element_type=F32
    ) * HD ** (-0.5)
    query_pos = query_first + jnp.arange(block_rows)
    key_pos = key_first + jnp.arange(key_span)
    distance = query_pos[:, None] - key_pos[None, :]
    allowed = (distance >= 0) & (distance < WIN) & (key_pos[None, :] >= 0)
    scores = jnp.where(allowed, scores, -1e30)
    row_peak = jnp.max(scores, axis=-1, keepdims=True)
    exp_scores = jnp.exp(scores - row_peak)
    attn_probs = (exp_scores / jnp.sum(exp_scores, axis=-1, keepdims=True)).astype(BF16)
    mixed_heads = jnp.einsum(
        "gjts,sgd->tgjd", attn_probs, value_split, preferred_element_type=F32
    )
    return mixed_heads.reshape(block_rows, -1).astype(BF16)


def ring(block):
    rows = block.shape[0] // 2
    got = {0: block}
    up, down = block, block
    for step in (1, 2, 3):
        up, down = moved(up, dz=1), moved(down, dz=-1)
        got[-step], got[step] = up, down
    low, high = moved(up[:rows], dz=1), moved(down[rows:], dz=-1)
    got[4] = (low, high)
    return got


def moved_x(block, dx):
    return lax.ppermute(block, "dp", [(x, (x + dx) % NX) for x in range(NX)])


def in_order(pieces, first, count):
    return lax.dynamic_slice_in_dim(jnp.stack(pieces + pieces), (count - first) % count, count, 0)


def tied_call(value, function_and_args):
    function, args = function_and_args
    value, args = tied((value, args))
    return value, lambda: function(*args)


def projection(attend, plan_of, out_weight, x, z, y, c):
    depth, width = out_weight.shape
    padded = jnp.pad(out_weight, ((0, 0), (0, NX * QUARTER - width)))
    kept = lax.dynamic_slice_in_dim(padded, x * QUARTER, QUARTER, 1)
    swapped, plan_of = tied_call(moved(kept, flip=True), plan_of)
    plan = plan_of()
    chip = in_order([kept, swapped], c, NC).reshape(-1, QUARTER)
    around = [chip, moved(chip, dy=-1), moved(chip, dy=2), moved(chip, dy=1)]
    plane = in_order(around, y, NY).reshape(-1, QUARTER)
    taken = plane.shape[0]
    plane, attend = tied_call(jnp.concatenate([plane, plan], 0), attend)
    parts = ring(plane)
    context = attend()
    parts[4] = jnp.concatenate(parts[4], 0)
    plans = {d: part[taken:] for d, part in parts.items()}

    rows = context.shape[0]
    up, down = moved_x(context, 1), moved_x(context, -1)
    low, high = moved_x(up[: rows // 2], 1), moved_x(down[rows // 2 :], -1)
    all_rows = jnp.concatenate([context, down, low, high, up], 0)
    all_rows = all_rows.reshape(NX * rows, NZ, -1).transpose(1, 0, 2)
    total = 0.0
    for d, part in parts.items():
        columns = lax.dynamic_index_in_dim(all_rows, (z + d) % NZ, 0, keepdims=False)
        total += jnp.dot(columns, part[:taken], preferred_element_type=F32)
    total = total.astype(BF16).reshape(NX, rows, QUARTER)
    quarters = [
        total[0],
        moved_x(total[3], -1),
        moved_x(total[2], 2),
        moved_x(total[1], 1),
    ]
    quarters = in_order(quarters, x, NX)
    return jnp.concatenate([quarters[i] for i in range(NX)], 1)[:, :width], plans


def ranks_of(expert_ids):
    rows = expert_ids.shape[0]
    experts = jnp.arange(NZ * NY * NC, dtype=jnp.int32)
    named = expert_ids[:, :, None] == experts
    marks = jnp.sum(named.astype(F32), axis=1).astype(BF16)
    steps = jnp.arange(rows)
    earlier = (steps[:, None] > steps[None, :]).astype(BF16)
    counts = jnp.dot(earlier, marks, preferred_element_type=F32)
    return jnp.sum(jnp.where(named, counts[:, None, :], 0.0), axis=2)


def call(body, outs, args, scratch=(), flops=0, limit=40):
    moved_bytes = sum(a.size * a.dtype.itemsize for a in (*args, *outs))
    return pl.pallas_call(
        body,
        out_shape=tuple(outs),
        in_specs=[pl.BlockSpec(memory_space=pltpu.VMEM)] * len(args),
        out_specs=tuple(pl.BlockSpec(memory_space=pltpu.VMEM) for _ in outs),
        scratch_shapes=list(scratch),
        compiler_params=pltpu.CompilerParams(vmem_limit_bytes=limit << 20),
        cost_estimate=pl.CostEstimate(
            flops=flops, bytes_accessed=moved_bytes, transcendentals=0
        ),
    )(*args)


def pick_rows(spots, blocks):
    pieces = [b if isinstance(b, tuple) else (b,) for b in blocks]
    flat = [piece for b in pieces for piece in b]
    count, (rows, width) = len(blocks), blocks[0].shape

    def body(spots_ref, *refs):
        ins, outs, whole = refs[: len(flat)], refs[len(flat) : -1], refs[-1]
        slot = lax.broadcasted_iota(jnp.int32, (SLOTS, rows), 0)
        at = 0
        for b in range(count):
            if len(pieces[b]) > 1:
                first = 0
                for piece in pieces[b]:
                    whole[first : first + piece.shape[0], :] = ins[at][...]
                    first, at = first + piece.shape[0], at + 1
                block = whole[...]
            else:
                block, at = ins[at][...], at + 1
            pick = jnp.zeros((SLOTS, rows), F32)
            for r in range(TOP):
                pick += jnp.where(spots_ref[b, r : r + 1, :] == slot, 1.0, 0.0)
            found = jnp.dot(pick.astype(BF16), block, preferred_element_type=F32).astype(BF16)
            for i in range(len(WAYS)):
                outs[i][b * CAP : (b + 1) * CAP, :] = found[i * CAP : (i + 1) * CAP]

    outs = [jax.ShapeDtypeStruct((count * CAP, width), BF16)] * len(WAYS)
    flops = 2 * count * SLOTS * rows * width
    return call(body, outs, [spots, *flat], [pltpu.VMEM((rows, width), BF16)], flops)


def run_expert(parts, gate_up, down):
    rows, width = parts[0].shape
    total, units = rows * len(parts), down.shape[0]
    wide = 512

    def body(gate_up_ref, down_ref, *refs):
        ins, outs = refs[: len(parts)], refs[len(parts) : -2]
        taken, projected = refs[-2:]
        for i, part in enumerate(ins):
            taken[i * rows : (i + 1) * rows, :] = part[...]
        for first in range(0, 2 * units, wide):
            last = min(first + wide, 2 * units)
            projected[:, first:last] = jnp.dot(
                taken[...], gate_up_ref[:, first:last], preferred_element_type=F32
            )
        for first in range(0, total, rows):
            gate = projected[first : first + rows, :units]
            up = projected[first : first + rows, units:]
            active = (up + 1.0) * gate * jax.nn.sigmoid(1.702 * gate)
            taken[first : first + rows, :] = active.astype(BF16)
        for first in range(0, width, wide):
            last = min(first + wide, width)
            made = jnp.dot(taken[...], down_ref[:, first:last], preferred_element_type=F32)
            made = made.astype(BF16)
            for i, out in enumerate(outs):
                out[:, first:last] = made[i * rows : (i + 1) * rows]

    outs = [jax.ShapeDtypeStruct((rows, width), BF16)] * len(parts)
    scratch = [pltpu.VMEM((total, width), BF16), pltpu.VMEM((total, 2 * units), F32)]
    flops = 6 * total * width * units
    return call(body, outs, [gate_up, down, *parts], scratch, flops)


def combine(spots, shares, parts, count):
    width = parts[0].shape[1]
    rows = spots.shape[2]

    def body(spots_ref, shares_ref, *refs):
        ins, outs, whole = refs[: len(parts)], refs[len(parts) : -1], refs[-1]
        slot = lax.broadcasted_iota(jnp.int32, (SLOTS, rows), 0)
        for b in range(count):
            for i, part in enumerate(ins):
                whole[i * CAP : (i + 1) * CAP, :] = part[b * CAP : (b + 1) * CAP, :]
            sums = 0.0
            for fine in range(2):
                share = jnp.zeros((SLOTS, rows), F32)
                for r in range(TOP):
                    here = spots_ref[b, r : r + 1, :] == slot
                    at = fine * TOP + r
                    share += jnp.where(here, shares_ref[b, at : at + 1, :], 0.0)
                sums += jnp.dot(share.T.astype(BF16), whole[...], preferred_element_type=F32)
            outs[b][...] = sums

    outs = [jax.ShapeDtypeStruct((rows, width), F32)] * count
    flops = 4 * count * SLOTS * rows * width
    return call(body, outs, [spots, shares, *parts], [pltpu.VMEM((SLOTS, width), BF16)], flops)


def shards(
    query_heads,
    key_heads,
    value_heads,
    out_weight,
    norm_gain,
    gate_up_weight,
    down_weight,
    expert_ids,
    route_weights,
):
    tok_rows = query_heads.shape[0]
    device_index = lax.axis_index("ep")
    z, y, c = device_index // (NY * NC), device_index // NC % NY, device_index % NC
    first_pos = device_index * tok_rows
    prev_keys, prev_values = from_behind((key_heads, value_heads), 1)
    keys_all = jnp.concatenate([prev_keys, key_heads], 0)
    values_all = jnp.concatenate([prev_values, value_heads], 0)

    def plan_of(ids, weights):
        coarse = lax.reduce_precision(weights, 8, 7)
        fine = lax.reduce_precision(weights - coarse, 8, 7)
        lanes = [
            jnp.concatenate([ids.astype(F32).T, ranks_of(ids).T], 0),
            jnp.concatenate([coarse.T, fine.T], 0),
        ]
        plan = jnp.concatenate([*lanes, jnp.zeros_like(lanes[0])], 1).astype(BF16)
        return jnp.concatenate([plan, jnp.zeros_like(plan)], 0)

    def attend(queries, keys, values):
        return window_attention(queries, keys, values, first_pos, first_pos - WIN)

    hidden, plans = projection(
        (attend, (query_heads, keys_all, values_all)),
        (plan_of, (expert_ids, route_weights)),
        out_weight,
        lax.axis_index("dp"),
        z,
        y,
        c,
    )

    near = [d for group in GROUPS for d in group]
    plans = jnp.stack([plans[d] for d in near]).astype(F32)
    shares = plans[:, : 2 * TOP, tok_rows : 2 * tok_rows]
    expert = plans[:, :TOP, :tok_rows].astype(jnp.int32) - z * (NY * NC)
    rank = plans[:, TOP : 2 * TOP, :tok_rows].astype(jnp.int32)
    way = (expert // NC - y) % NY * NC + (expert % NC ^ c)
    here = (expert >= 0) & (expert < NY * NC)
    spots = jnp.where(here, way * CAP + rank, -1)

    hidden_f = lax.optimization_barrier(hidden).astype(F32)
    scale_rms = lax.rsqrt(jnp.mean(hidden_f * hidden_f, axis=-1, keepdims=True) + 1e-05)
    normed = (hidden_f * scale_rms * norm_gain).astype(BF16)

    near_count, half = len(GROUPS[0]), tok_rows // 2
    every = range(len(WAYS))

    def spread(rows, lots, back=False):
        sign = -1 if back else 1
        return {i: moved(rows[i], dy=sign * WAYS[i][0], flip=WAYS[i][1]) for i in lots}

    up, down = moved(normed, dz=1), moved(normed, dz=-1)
    held = [normed, down, up]
    up, down = moved(up, dz=1), moved(down, dz=-1)
    rows = pick_rows(spots[:near_count], [*held, down, up])
    up, down, rows = tied((up, down, rows))
    up, down, got = tied((moved(up, dz=1), moved(down, dz=-1), spread(rows, EARLY)))
    up, down, rows = tied((up, down, rows))
    held = [down, up]
    low, high, late = tied((moved(up[:half], dz=1), moved(down[half:], dz=-1), spread(rows, LATE)))
    got.update(late)
    far_rows = pick_rows(spots[near_count:], [*held, (low, high)])
    far_got = spread(far_rows, every)
    far_made = run_expert([far_got[i] for i in every], gate_up_weight[0], down_weight[0])
    far_made, got = tied((far_made, got))
    far_back = spread(far_made, every, back=True)
    made = run_expert([got[i] for i in every], gate_up_weight[0], down_weight[0])
    sums = combine(spots[near_count:], shares[near_count:], [far_back[i] for i in every], len(GROUPS[1]))
    sums, made = tied((sums, made))
    partial = dict(zip(GROUPS[1], sums))
    up = moved(partial[4][half:].astype(BF16), dz=1)
    down = moved(partial[4][:half].astype(BF16), dz=-1)
    up, down, back, made = tied((up, down, spread(made, EARLY, back=True), made))
    up = partial[3] + jnp.pad(up.astype(F32), ((half, 0), (0, 0)))
    down = partial[-3] + jnp.pad(down.astype(F32), ((0, half), (0, 0)))
    up, down = moved(up.astype(BF16), dz=1), moved(down.astype(BF16), dz=-1)
    up, down, late = tied((up, down, spread(made, LATE, back=True)))
    back.update(late)
    sums = combine(spots[:near_count], shares[:near_count], [back[i] for i in every], near_count)
    partial.update(zip(GROUPS[0], sums))
    up, down = up.astype(F32) + partial[2], down.astype(F32) + partial[-2]
    for step in (1, 0):
        up = moved(up.astype(BF16), dz=1).astype(F32)
        down = moved(down.astype(BF16), dz=-1).astype(F32)
        if step:
            up, down = up + partial[step], down + partial[-step]
    return (hidden_f + (partial[0] + up + down)).astype(BF16)


def solution(mesh):
    placed = (
        P(("dp", "ep"), None),
        P(("dp", "ep"), None),
        P(("dp", "ep"), None),
        P("ep", None),
        P(),
        P("ep", None, None),
        P("ep", None, None),
        P(("dp", "ep"), None),
        P(("dp", "ep"), None),
    )
    return jax.shard_map(
        shards, mesh=mesh, in_specs=placed, out_specs=P(("dp", "ep"), None), check_vma=False
    )
```

```python
import jax
import jax.numpy as jnp
from jax import lax
from jax.experimental import pallas as pl
from jax.experimental.pallas import tpu as pltpu
from jax.sharding import PartitionSpec as P

HD = 64
WIN = 128
NX, NZ, NY, NC = 4, 8, 4, 2
CAP = 16
QUARTER = 384
SLOTS = NY * NC * CAP
GROUPS = ((0, 1, -1, 2, -2), (3, -3, 4))
WAYS = tuple((dy, flip) for dy in range(NY) for flip in range(NC))
TOP = 4
BF16 = jnp.bfloat16
F32 = jnp.float32


def tied(values):
    return lax.optimization_barrier(values)


def index_of(z, y, c):
    return ((z % NZ) * NY + y % NY) * NC + c


def moved(block, dz=0, dy=0, flip=False):
    if not (dz or dy or flip):
        return block
    route = [
        (index_of(z, y, c), index_of(z + dz, y + dy, 1 - c if flip else c))
        for z in range(NZ)
        for y in range(NY)
        for c in range(NC)
    ]
    return lax.ppermute(block, "ep", route)


def from_behind(block, distance):
    devices = range(NZ * NY * NC)
    route = [(i - distance, i) for i in devices if i - distance in devices]
    return lax.ppermute(block, "ep", route)


def window_attention(query_block, key_block, value_block, query_first, key_first):
    block_rows = query_block.shape[0]
    key_span = key_block.shape[0]
    kv_heads = key_block.shape[1] // HD
    group_size = query_block.shape[1] // key_block.shape[1]
    query_split = query_block.reshape(block_rows, kv_heads, group_size, HD)
    key_split = key_block.reshape(key_span, kv_heads, HD)
    value_split = value_block.reshape(key_span, kv_heads, HD)
    scores = jnp.einsum(
        "tgjd,sgd->gjts", query_split, key_split, preferred_element_type=F32
    ) * HD ** (-0.5)
    query_pos = query_first + jnp.arange(block_rows)
    key_pos = key_first + jnp.arange(key_span)
    distance = query_pos[:, None] - key_pos[None, :]
    allowed = (distance >= 0) & (distance < WIN) & (key_pos[None, :] >= 0)
    scores = jnp.where(allowed, scores, -1e30)
    row_peak = jnp.max(scores, axis=-1, keepdims=True)
    exp_scores = jnp.exp(scores - row_peak)
    attn_probs = (exp_scores / jnp.sum(exp_scores, axis=-1, keepdims=True)).astype(BF16)
    mixed_heads = jnp.einsum(
        "gjts,sgd->tgjd", attn_probs, value_split, preferred_element_type=F32
    )
    return mixed_heads.reshape(block_rows, -1).astype(BF16)


def moved_x(block, dx):
    return lax.ppermute(block, "dp", [(x, (x + dx) % NX) for x in range(NX)])


def in_order(pieces, first, count):
    return lax.dynamic_slice_in_dim(jnp.stack(pieces + pieces), (count - first) % count, count, 0)


def tied_call(value, function_and_args):
    function, args = function_and_args
    value, args = tied((value, args))
    return value, lambda: function(*args)


def projection(attend, plan_of, out_weight, x, z, y, c):
    depth, width = out_weight.shape
    padded = jnp.pad(out_weight, ((0, 0), (0, NX * QUARTER - width)))
    kept = lax.dynamic_slice_in_dim(padded, x * QUARTER, QUARTER, 1)
    swapped, plan_of = tied_call(moved(kept, flip=True), plan_of)
    plan = plan_of()
    chip = in_order([kept, swapped], c, NC).reshape(-1, QUARTER)
    around = [chip, moved(chip, dy=-1), moved(chip, dy=2), moved(chip, dy=1)]
    plane = in_order(around, y, NY).reshape(-1, QUARTER)
    taken = plane.shape[0]
    plane, attend = tied_call(jnp.concatenate([plane, plan], 0), attend)
    same_line = [[index_of(i, j, k) for i in range(NZ)] for j in range(NY) for k in range(NC)]
    parts = lax.all_gather(plane, "ep", axis=0, axis_index_groups=same_line)
    context = attend()
    rows = context.shape[0]
    up, down = moved_x(context, 1), moved_x(context, -1)
    low, high = moved_x(up[: rows // 2], 1), moved_x(down[rows // 2 :], -1)
    quarters = multiply(parts, [context, down, (low, high), up])
    quarters = [
        quarters[0],
        moved_x(quarters[3], -1),
        moved_x(quarters[2], 2),
        moved_x(quarters[1], 1),
    ]
    return quarters, parts[:, NY * NC * depth :]


def multiply(weight, contexts):
    pieces = [b if isinstance(b, tuple) else (b,) for b in contexts]
    flat = [piece for b in pieces for piece in b]
    rows, depth = contexts[0].shape
    share = depth // NZ

    def body(weight_ref, *refs):
        ins, outs = refs[: len(flat)], refs[len(flat) :]
        at = 0
        for out, b in zip(outs, pieces):
            first = 0
            for piece in b:
                total = jnp.zeros((piece.shape[0], QUARTER), F32)
                for i in range(NZ):
                    total += jnp.dot(
                        ins[at][:, i * share : (i + 1) * share],
                        weight_ref[i, :share, :],
                        preferred_element_type=F32,
                    )
                out[first : first + piece.shape[0], :] = total.astype(BF16)
                first, at = first + piece.shape[0], at + 1

    outs = [jax.ShapeDtypeStruct((rows, QUARTER), BF16)] * len(pieces)
    return call(body, outs, [weight, *flat], (), 2 * len(pieces) * rows * depth * QUARTER)


def join_and_norm(quarters, gain, x):
    rows, width = quarters[0].shape[0], gain.shape[0]

    def body(x_ref, gain_ref, *refs):
        ins, (hidden_ref, normed_ref, whole) = refs[:NX], refs[NX:]
        for k, piece in enumerate(ins):
            first = pl.multiple_of((x_ref[0] + k) % NX * QUARTER, QUARTER)
            whole[:, pl.ds(first, QUARTER)] = piece[...]
        hidden = whole[:, :width]
        hidden_ref[...] = hidden
        hidden = hidden.astype(F32)
        scale = lax.rsqrt(jnp.mean(hidden * hidden, axis=-1, keepdims=True) + 1e-05)
        normed_ref[...] = (hidden * scale * gain_ref[...]).astype(BF16)

    in_vmem = pl.BlockSpec(memory_space=pltpu.VMEM)
    return pl.pallas_call(
        body,
        out_shape=(jax.ShapeDtypeStruct((rows, width), BF16),) * 2,
        in_specs=[pl.BlockSpec(memory_space=pltpu.SMEM)] + [in_vmem] * (NX + 1),
        out_specs=(in_vmem,) * 2,
        scratch_shapes=[pltpu.VMEM((rows, NX * QUARTER), BF16)],
        compiler_params=pltpu.CompilerParams(vmem_limit_bytes=16 << 20),
    )(x.reshape(1), gain.reshape(1, -1), *quarters)


def ranks_of(expert_ids):
    rows = expert_ids.shape[0]
    experts = jnp.arange(NZ * NY * NC, dtype=jnp.int32)
    named = expert_ids[:, :, None] == experts
    marks = jnp.sum(named.astype(F32), axis=1).astype(BF16)
    steps = jnp.arange(rows)
    earlier = (steps[:, None] > steps[None, :]).astype(BF16)
    counts = jnp.dot(earlier, marks, preferred_element_type=F32)
    return jnp.sum(jnp.where(named, counts[:, None, :], 0.0), axis=2)


def call(body, outs, args, scratch=(), flops=0, limit=40):
    moved_bytes = sum(a.size * a.dtype.itemsize for a in (*args, *outs))
    return pl.pallas_call(
        body,
        out_shape=tuple(outs),
        in_specs=[pl.BlockSpec(memory_space=pltpu.VMEM)] * len(args),
        out_specs=tuple(pl.BlockSpec(memory_space=pltpu.VMEM) for _ in outs),
        scratch_shapes=list(scratch),
        compiler_params=pltpu.CompilerParams(vmem_limit_bytes=limit << 20),
        cost_estimate=pl.CostEstimate(
            flops=flops, bytes_accessed=moved_bytes, transcendentals=0
        ),
    )(*args)


def pick_rows(spots, blocks, joined=False):
    pieces = [b if isinstance(b, tuple) else (b,) for b in blocks]
    flat = [piece for b in pieces for piece in b]
    count, (rows, width) = len(blocks), blocks[0].shape

    def body(spots_ref, *refs):
        ins, outs, whole = refs[: len(flat)], refs[len(flat) : -1], refs[-1]
        slot = lax.broadcasted_iota(jnp.int32, (SLOTS, rows), 0)
        at = 0
        for b in range(count):
            if len(pieces[b]) > 1:
                first = 0
                for piece in pieces[b]:
                    whole[first : first + piece.shape[0], :] = ins[at][...]
                    first, at = first + piece.shape[0], at + 1
                block = whole[...]
            else:
                block, at = ins[at][...], at + 1
            pick = jnp.zeros((SLOTS, rows), F32)
            for r in range(TOP):
                pick += jnp.where(spots_ref[b, r : r + 1, :] == slot, 1.0, 0.0)
            found = jnp.dot(pick.astype(BF16), block, preferred_element_type=F32).astype(BF16)
            for i in range(len(WAYS)):
                to, first = (outs[0], i * count * CAP) if joined else (outs[i], 0)
                first += b * CAP
                to[first : first + CAP, :] = found[i * CAP : (i + 1) * CAP]

    outs = [jax.ShapeDtypeStruct((count * CAP, width), BF16)] * len(WAYS)
    if joined:
        outs = [jax.ShapeDtypeStruct((len(WAYS) * count * CAP, width), BF16)]
    flops = 2 * count * SLOTS * rows * width
    return call(body, outs, [spots, *flat], [pltpu.VMEM((rows, width), BF16)], flops)


def run_expert(parts, gate_up, down):
    rows, width = parts[0].shape
    total, units = rows * len(parts), down.shape[0]
    wide, tall = 512, 128

    def body(gate_up_ref, down_ref, *refs):
        ins, outs = refs[: len(parts)], refs[len(parts) : -2]
        taken, projected = refs[-2:]
        for i, part in enumerate(ins):
            taken[i * rows : (i + 1) * rows, :] = part[...]
        for first in range(0, 2 * units, wide):
            last = min(first + wide, 2 * units)
            projected[:, first:last] = jnp.dot(
                taken[...], gate_up_ref[:, first:last], preferred_element_type=F32
            )
        for first in range(0, total, tall):
            gate = projected[first : first + tall, :units]
            up = projected[first : first + tall, units:]
            active = (up + 1.0) * gate * jax.nn.sigmoid(1.702 * gate)
            taken[first : first + tall, :] = active.astype(BF16)
        for first in range(0, width, wide):
            last = min(first + wide, width)
            made = jnp.dot(taken[...], down_ref[:, first:last], preferred_element_type=F32)
            made = made.astype(BF16)
            for i, out in enumerate(outs):
                out[:, first:last] = made[i * rows : (i + 1) * rows]

    outs = [jax.ShapeDtypeStruct((rows, width), BF16)] * len(parts)
    scratch = [pltpu.VMEM((total, width), BF16), pltpu.VMEM((total, 2 * units), F32)]
    flops = 6 * total * width * units
    return call(body, outs, [gate_up, down, *parts], scratch, flops)


def combine(spots, shares, parts, count):
    width = parts[0].shape[1]
    rows = spots.shape[2]

    def body(spots_ref, shares_ref, *refs):
        ins, outs, whole = refs[: len(parts)], refs[len(parts) : -1], refs[-1]
        slot = lax.broadcasted_iota(jnp.int32, (SLOTS, rows), 0)
        for b in range(count):
            for i in range(len(WAYS)):
                part, first = (ins[i], 0) if len(parts) > 1 else (ins[0], i * count * CAP)
                first += b * CAP
                whole[i * CAP : (i + 1) * CAP, :] = part[first : first + CAP, :]
            sums = 0.0
            for fine in range(2):
                share = jnp.zeros((SLOTS, rows), F32)
                for r in range(TOP):
                    here = spots_ref[b, r : r + 1, :] == slot
                    at = fine * TOP + r
                    share += jnp.where(here, shares_ref[b, at : at + 1, :], 0.0)
                sums += jnp.dot(share.T.astype(BF16), whole[...], preferred_element_type=F32)
            outs[b][...] = sums

    outs = [jax.ShapeDtypeStruct((rows, width), F32)] * count
    flops = 4 * count * SLOTS * rows * width
    return call(body, outs, [spots, shares, *parts], [pltpu.VMEM((SLOTS, width), BF16)], flops)


def shards(
    query_heads,
    key_heads,
    value_heads,
    out_weight,
    norm_gain,
    gate_up_weight,
    down_weight,
    expert_ids,
    route_weights,
):
    tok_rows = query_heads.shape[0]
    device_index = lax.axis_index("ep")
    z, y, c = device_index // (NY * NC), device_index // NC % NY, device_index % NC
    first_pos = device_index * tok_rows
    prev_keys, prev_values = from_behind((key_heads, value_heads), 1)
    keys_all = jnp.concatenate([prev_keys, key_heads], 0)
    values_all = jnp.concatenate([prev_values, value_heads], 0)

    def plan_of(ids, weights):
        coarse = lax.reduce_precision(weights, 8, 7)
        fine = lax.reduce_precision(weights - coarse, 8, 7)
        lanes = [
            jnp.concatenate([ids.astype(F32).T, ranks_of(ids).T], 0),
            jnp.concatenate([coarse.T, fine.T], 0),
        ]
        plan = jnp.concatenate([*lanes, jnp.zeros_like(lanes[0])], 1).astype(BF16)
        return jnp.concatenate([plan, jnp.zeros_like(plan)], 0)

    def attend(queries, keys, values):
        return window_attention(queries, keys, values, first_pos, first_pos - WIN)

    x = lax.axis_index("dp")
    quarters, plans = projection(
        (attend, (query_heads, keys_all, values_all)),
        (plan_of, (expert_ids, route_weights)),
        out_weight,
        x,
        z,
        y,
        c,
    )
    hidden, normed = join_and_norm(quarters, norm_gain, x)

    plans = lax.dynamic_slice_in_dim(jnp.concatenate([plans, plans], 0), z, NZ, 0)
    plans = jnp.stack([plans[d % NZ] for group in GROUPS for d in group]).astype(F32)
    shares = plans[:, : 2 * TOP, tok_rows : 2 * tok_rows]
    expert = plans[:, :TOP, :tok_rows].astype(jnp.int32) - z * (NY * NC)
    rank = plans[:, TOP : 2 * TOP, :tok_rows].astype(jnp.int32)
    way = (expert // NC - y) % NY * NC + (expert % NC ^ c)
    here = (expert >= 0) & (expert < NY * NC)
    near_spots = jnp.where(here, expert * CAP + rank, -1)[: len(GROUPS[0])]
    far_spots = jnp.where(here, way * CAP + rank, -1)[len(GROUPS[0]) :]

    near_count, half = len(GROUPS[0]), tok_rows // 2
    every = range(len(WAYS))

    def spread(rows, lots, back=False):
        sign = -1 if back else 1
        return {i: moved(rows[i], dy=sign * WAYS[i][0], flip=WAYS[i][1]) for i in lots}

    same_plane = [[index_of(i, j, k) for j in range(NY) for k in range(NC)] for i in range(NZ)]

    def exchange(rows):
        rows = rows.reshape(NY * NC, -1, rows.shape[1])
        rows = lax.all_to_all(
            rows, "ep", split_axis=0, concat_axis=0, tiled=True, axis_index_groups=same_plane
        )
        return rows.reshape(-1, rows.shape[2])

    up, down = moved(normed, dz=1), moved(normed, dz=-1)
    held = [normed, down, up]
    up, down = moved(up, dz=1), moved(down, dz=-1)
    [rows] = pick_rows(near_spots, [*held, down, up], joined=True)
    up, down, rows = tied((up, down, rows))
    got = exchange(rows)
    up, down = moved(up, dz=1), moved(down, dz=-1)
    held = [down, up]
    low, high = moved(up[:half], dz=1), moved(down[half:], dz=-1)
    far_rows = pick_rows(far_spots, [*held, (low, high)])
    far_got = spread(far_rows, every)
    [made] = run_expert([got], gate_up_weight[0], down_weight[0])
    far_got, made = tied((far_got, made))
    far_made = run_expert([far_got[i] for i in every], gate_up_weight[0], down_weight[0])
    far_back = spread(far_made, every, back=True)
    sums = combine(far_spots, shares[near_count:], [far_back[i] for i in every], len(GROUPS[1]))
    partial = dict(zip(GROUPS[1], sums))
    *far_made, made = tied((*far_made, made))
    back = exchange(made)
    up = moved(partial[4][half:].astype(BF16), dz=1)
    down = moved(partial[4][:half].astype(BF16), dz=-1)
    up = partial[3] + jnp.pad(up.astype(F32), ((half, 0), (0, 0)))
    down = partial[-3] + jnp.pad(down.astype(F32), ((0, half), (0, 0)))
    up, down = moved(up.astype(BF16), dz=1), moved(down.astype(BF16), dz=-1)
    sums = combine(near_spots, shares[:near_count], [back], near_count)
    partial.update(zip(GROUPS[0], sums))
    up, down = up.astype(F32) + partial[2], down.astype(F32) + partial[-2]
    for step in (1, 0):
        up = moved(up.astype(BF16), dz=1).astype(F32)
        down = moved(down.astype(BF16), dz=-1).astype(F32)
        if step:
            up, down = up + partial[step], down + partial[-step]
    return (hidden.astype(F32) + (partial[0] + up + down)).astype(BF16)


def solution(mesh):
    placed = (
        P(("dp", "ep"), None),
        P(("dp", "ep"), None),
        P(("dp", "ep"), None),
        P("ep", None),
        P(),
        P("ep", None, None),
        P("ep", None, None),
        P(("dp", "ep"), None),
        P(("dp", "ep"), None),
    )
    return jax.shard_map(
        shards, mesh=mesh, in_specs=placed, out_specs=P(("dp", "ep"), None), check_vma=False
    )
```

```python
import jax
import jax.numpy as jnp
from jax import lax
from jax.experimental import pallas as pl
from jax.experimental.pallas import tpu as pltpu
from jax.sharding import PartitionSpec as P

HD = 64
WIN = 128
NX, NZ, NY, NC = 4, 8, 4, 2
CAP = 16
QUARTER = 384
SLOTS = NY * NC * CAP
GROUPS = ((0, 1, -1, 2, -2), (3, -3, 4))
WAYS = tuple((dy, flip) for dy in range(NY) for flip in range(NC))
TOP = 4
BF16 = jnp.bfloat16
F32 = jnp.float32


def tied(values):
    return lax.optimization_barrier(values)


def index_of(z, y, c):
    return ((z % NZ) * NY + y % NY) * NC + c


def moved(block, dz=0, dy=0, flip=False):
    if not (dz or dy or flip):
        return block
    route = [
        (index_of(z, y, c), index_of(z + dz, y + dy, 1 - c if flip else c))
        for z in range(NZ)
        for y in range(NY)
        for c in range(NC)
    ]
    return lax.ppermute(block, "ep", route)


def from_behind(block, distance):
    devices = range(NZ * NY * NC)
    route = [(i - distance, i) for i in devices if i - distance in devices]
    return lax.ppermute(block, "ep", route)


def window_attention(query_block, key_block, value_block, query_first, key_first):
    block_rows = query_block.shape[0]
    key_span = key_block.shape[0]
    kv_heads = key_block.shape[1] // HD
    group_size = query_block.shape[1] // key_block.shape[1]
    query_split = query_block.reshape(block_rows, kv_heads, group_size, HD)
    key_split = key_block.reshape(key_span, kv_heads, HD)
    value_split = value_block.reshape(key_span, kv_heads, HD)
    scores = jnp.einsum(
        "tgjd,sgd->gjts", query_split, key_split, preferred_element_type=F32
    ) * HD ** (-0.5)
    query_pos = query_first + jnp.arange(block_rows)
    key_pos = key_first + jnp.arange(key_span)
    distance = query_pos[:, None] - key_pos[None, :]
    allowed = (distance >= 0) & (distance < WIN) & (key_pos[None, :] >= 0)
    scores = jnp.where(allowed, scores, -1e30)
    row_peak = jnp.max(scores, axis=-1, keepdims=True)
    exp_scores = jnp.exp(scores - row_peak)
    attn_probs = (exp_scores / jnp.sum(exp_scores, axis=-1, keepdims=True)).astype(BF16)
    mixed_heads = jnp.einsum(
        "gjts,sgd->tgjd", attn_probs, value_split, preferred_element_type=F32
    )
    return mixed_heads.reshape(block_rows, -1).astype(BF16)


def moved_x(block, dx):
    return lax.ppermute(block, "dp", [(x, (x + dx) % NX) for x in range(NX)])


def in_order(pieces, first, count):
    return lax.dynamic_slice_in_dim(jnp.stack(pieces + pieces), (count - first) % count, count, 0)


def projection(attend, before_of, plan_of, out_weight, x, z, y, c):
    depth, width = out_weight.shape
    padded = jnp.pad(out_weight, ((0, 0), (0, NX * QUARTER - width)))
    kept = lax.dynamic_slice_in_dim(padded, x * QUARTER, QUARTER, 1)
    (attend, queries), (before_of, before), (plan_of, plan) = attend, before_of, plan_of
    swapped, before, plan = tied((moved(kept, flip=True), before, plan))
    plan, span = plan_of(*plan), before_of(*before)
    chip = in_order([kept, swapped], c, NC).reshape(-1, QUARTER)
    around = [chip, moved(chip, dy=-1), moved(chip, dy=2), moved(chip, dy=1)]
    plane = in_order(around, y, NY).reshape(-1, QUARTER)
    taken = plane.shape[0]
    plane, queries = tied((jnp.concatenate([plane, plan], 0), queries))
    split = plane.shape[0] // 2 // 16 * 16
    up, down, context = tied(
        (moved(plane, dz=1), moved(plane, dz=-1), attend(queries, *span))
    )
    parts = {0: plane, -1: up, 1: down}
    for step in (2, 3):
        up, down = moved(up, dz=1), moved(down, dz=-1)
        parts[-step], parts[step] = up, down
    parts[4] = (moved(up[:split], dz=1), moved(down[split:], dz=-1))
    rows = context.shape[0]
    up, down = moved_x(context, 1), moved_x(context, -1)
    low, high = moved_x(up[: rows // 2], 1), moved_x(down[rows // 2 :], -1)
    *quarters, spots, shares = multiply(parts, [context, down, low, high, up], (z, y, c))
    quarters = [
        quarters[0],
        moved_x(quarters[3], -1),
        moved_x(quarters[2], 2),
        moved_x(quarters[1], 1),
    ]
    return quarters, spots, shares


def multiply(parts, contexts, place):
    order = [d for group in GROUPS for d in group]
    pieces = [parts[d] if isinstance(parts[d], tuple) else (parts[d],) for d in order]
    flat = [piece for b in pieces for piece in b]
    taken, depth = parts[0].shape[0], contexts[0].shape[1]
    share = depth // NZ
    rows = contexts[0].shape[0]
    tall = sum(b.shape[0] for b in contexts)

    def body(place_ref, *refs):
        weights, ins = refs[: len(flat)], refs[len(flat) : len(flat) + len(contexts)]
        *outs, spots_ref, shares_ref, whole, joined = refs[len(flat) + len(contexts) :]
        z, y, c = place_ref[0], place_ref[1], place_ref[2]
        first = 0
        for piece in ins:
            whole[first : first + piece.shape[0], :] = piece[...]
            first += piece.shape[0]
        total = jnp.zeros((tall, QUARTER), F32)
        at = 0
        for k, d in enumerate(order):
            part = weights[at]
            if len(pieces[k]) > 1:
                first = 0
                for piece in pieces[k]:
                    joined[first : first + piece.shape[0], :] = weights[at][...]
                    first, at = first + piece.shape[0], at + 1
                part = joined
            else:
                at += 1
            column = pl.multiple_of(lax.rem(z + (d + NZ), NZ) * share, share)
            total += jnp.dot(
                whole[:, pl.ds(column, share)], part[:share, :], preferred_element_type=F32
            )
            plan = part[share : share + 2 * TOP, :].astype(F32)
            expert = plan[:TOP, :rows].astype(jnp.int32) - z * (NY * NC)
            rank = plan[TOP:, :rows].astype(jnp.int32)
            way = expert
            if k >= len(GROUPS[0]):
                way = (((expert >> 1) - y) & (NY - 1)) * NC + ((expert & 1) ^ c)
            here = (expert >= 0) & (expert < NY * NC)
            spots_ref[k] = jnp.where(here, way * CAP + rank, -1)
            shares_ref[k] = plan[:, rows : 2 * rows]
        total = total.astype(BF16)
        for k, out in enumerate(outs):
            out[...] = total[k * rows : (k + 1) * rows]

    outs = [jax.ShapeDtypeStruct((rows, QUARTER), BF16)] * NX
    outs.append(jax.ShapeDtypeStruct((NZ, TOP, rows), jnp.int32))
    outs.append(jax.ShapeDtypeStruct((NZ, 2 * TOP, rows), F32))
    scratch = [pltpu.VMEM((tall, depth), BF16), pltpu.VMEM((taken, QUARTER), BF16)]
    args = [jnp.stack(place), *flat, *contexts]
    return call(body, outs, args, scratch, 2 * tall * depth * QUARTER, scalars=1)


def join_and_norm(quarters, gain, x):
    rows, width = quarters[0].shape[0], gain.shape[0]

    def body(x_ref, gain_ref, *refs):
        ins, (hidden_ref, normed_ref, whole) = refs[:NX], refs[NX:]
        for k, piece in enumerate(ins):
            first = pl.multiple_of((x_ref[0] + k) % NX * QUARTER, QUARTER)
            whole[:, pl.ds(first, QUARTER)] = piece[...]
        hidden = whole[:, :width]
        hidden_ref[...] = hidden
        hidden = hidden.astype(F32)
        scale = lax.rsqrt(jnp.mean(hidden * hidden, axis=-1, keepdims=True) + 1e-05)
        normed_ref[...] = (hidden * scale * gain_ref[...]).astype(BF16)

    in_vmem = pl.BlockSpec(memory_space=pltpu.VMEM)
    return pl.pallas_call(
        body,
        out_shape=(jax.ShapeDtypeStruct((rows, width), BF16),) * 2,
        in_specs=[pl.BlockSpec(memory_space=pltpu.SMEM)] + [in_vmem] * (NX + 1),
        out_specs=(in_vmem,) * 2,
        scratch_shapes=[pltpu.VMEM((rows, NX * QUARTER), BF16)],
        compiler_params=pltpu.CompilerParams(vmem_limit_bytes=16 << 20),
    )(x.reshape(1), gain.reshape(1, -1), *quarters)


def ranks_of(expert_ids):
    rows = expert_ids.shape[0]
    experts = jnp.arange(NZ * NY * NC, dtype=jnp.int32)
    named = expert_ids[:, :, None] == experts
    marks = jnp.sum(named.astype(F32), axis=1).astype(BF16)
    steps = jnp.arange(rows)
    earlier = (steps[:, None] > steps[None, :]).astype(BF16)
    counts = jnp.dot(earlier, marks, preferred_element_type=F32)
    return jnp.sum(jnp.where(named, counts[:, None, :], 0.0), axis=2)


def call(body, outs, args, scratch=(), flops=0, limit=40, scalars=0):
    moved_bytes = sum(a.size * a.dtype.itemsize for a in (*args, *outs))
    return pl.pallas_call(
        body,
        out_shape=tuple(outs),
        in_specs=[pl.BlockSpec(memory_space=pltpu.SMEM)] * scalars
        + [pl.BlockSpec(memory_space=pltpu.VMEM)] * (len(args) - scalars),
        out_specs=tuple(pl.BlockSpec(memory_space=pltpu.VMEM) for _ in outs),
        scratch_shapes=list(scratch),
        compiler_params=pltpu.CompilerParams(vmem_limit_bytes=limit << 20),
        cost_estimate=pl.CostEstimate(
            flops=flops, bytes_accessed=moved_bytes, transcendentals=0
        ),
    )(*args)


def pick_rows(spots, blocks, joined=False):
    pieces = [b if isinstance(b, tuple) else (b,) for b in blocks]
    flat = [piece for b in pieces for piece in b]
    count, (rows, width) = len(blocks), blocks[0].shape

    def body(spots_ref, *refs):
        ins, outs, whole = refs[: len(flat)], refs[len(flat) : -1], refs[-1]
        slot = lax.broadcasted_iota(jnp.int32, (SLOTS, rows), 0)
        at = 0
        for b in range(count):
            if len(pieces[b]) > 1:
                first = 0
                for piece in pieces[b]:
                    whole[first : first + piece.shape[0], :] = ins[at][...]
                    first, at = first + piece.shape[0], at + 1
                block = whole[...]
            else:
                block, at = ins[at][...], at + 1
            pick = jnp.zeros((SLOTS, rows), F32)
            for r in range(TOP):
                pick += jnp.where(spots_ref[b, r : r + 1, :] == slot, 1.0, 0.0)
            found = jnp.dot(pick.astype(BF16), block, preferred_element_type=F32).astype(BF16)
            for i in range(len(WAYS)):
                to, first = (outs[0], i * count * CAP) if joined else (outs[i], 0)
                first += b * CAP
                to[first : first + CAP, :] = found[i * CAP : (i + 1) * CAP]

    outs = [jax.ShapeDtypeStruct((count * CAP, width), BF16)] * len(WAYS)
    if joined:
        outs = [jax.ShapeDtypeStruct((len(WAYS) * count * CAP, width), BF16)]
    flops = 2 * count * SLOTS * rows * width
    return call(body, outs, [spots, *flat], [pltpu.VMEM((rows, width), BF16)], flops)


def run_expert(parts, gate_up, down):
    rows, width = parts[0].shape
    total, units = rows * len(parts), down.shape[0]
    wide, tall = 512, 128
    ups, downs = pl.cdiv(2 * units, wide), pl.cdiv(width, wide)

    def body(gate_up_ref, down_ref, *refs):
        ins, outs = refs[: len(parts)], refs[len(parts) : -2]
        taken, projected = refs[-2:]
        step = pl.program_id(0)

        @pl.when(step == 0)
        def _():
            for i, part in enumerate(ins):
                taken[i * rows : (i + 1) * rows, :] = part[...]

        @pl.when(step < ups)
        def _():
            first = pl.multiple_of(step * wide, wide)
            projected[:, pl.ds(first, wide)] = jnp.dot(
                taken[...], gate_up_ref[...], preferred_element_type=F32
            )

        @pl.when(step == ups)
        def _():
            for first in range(0, total, tall):
                gate = projected[first : first + tall, :units]
                up = projected[first : first + tall, units : 2 * units]
                active = (up + 1.0) * gate * jax.nn.sigmoid(1.702 * gate)
                taken[first : first + tall, :] = active.astype(BF16)

        for at in range(downs):

            @pl.when(step == ups + at)
            def _(first=at * wide):
                last = min(first + wide, width)
                made = jnp.dot(
                    taken[...], down_ref[:, : last - first], preferred_element_type=F32
                ).astype(BF16)
                for i, out in enumerate(outs):
                    out[:, first:last] = made[i * rows : (i + 1) * rows]

    outs = [jax.ShapeDtypeStruct((rows, width), BF16)] * len(parts)
    in_vmem = pl.BlockSpec(memory_space=pltpu.VMEM)
    return pl.pallas_call(
        body,
        grid=(ups + downs,),
        out_shape=tuple(outs),
        in_specs=[
            pl.BlockSpec((width, wide), lambda i: (0, jnp.minimum(i, ups - 1))),
            pl.BlockSpec((units, wide), lambda i: (0, jnp.maximum(i - ups, 0))),
        ]
        + [in_vmem] * len(parts),
        out_specs=(in_vmem,) * len(outs),
        scratch_shapes=[
            pltpu.VMEM((total, width), BF16),
            pltpu.VMEM((total, ups * wide), F32),
        ],
        compiler_params=pltpu.CompilerParams(vmem_limit_bytes=40 << 20),
        cost_estimate=pl.CostEstimate(
            flops=6 * total * width * units,
            bytes_accessed=6 * width * units + 4 * total * width,
            transcendentals=0,
        ),
    )(gate_up, down, *parts)


def combine(spots, shares, parts, count):
    width = parts[0].shape[1]
    rows = spots.shape[2]

    def body(spots_ref, shares_ref, *refs):
        ins, outs, whole = refs[: len(parts)], refs[len(parts) : -1], refs[-1]
        slot = lax.broadcasted_iota(jnp.int32, (SLOTS, rows), 0)
        for b in range(count):
            for i in range(len(WAYS)):
                part, first = (ins[i], 0) if len(parts) > 1 else (ins[0], i * count * CAP)
                first += b * CAP
                whole[i * CAP : (i + 1) * CAP, :] = part[first : first + CAP, :]
            sums = 0.0
            for fine in range(2):
                share = jnp.zeros((SLOTS, rows), F32)
                for r in range(TOP):
                    here = spots_ref[b, r : r + 1, :] == slot
                    at = fine * TOP + r
                    share += jnp.where(here, shares_ref[b, at : at + 1, :], 0.0)
                sums += jnp.dot(share.T.astype(BF16), whole[...], preferred_element_type=F32)
            outs[b][...] = sums

    outs = [jax.ShapeDtypeStruct((rows, width), F32)] * count
    flops = 4 * count * SLOTS * rows * width
    return call(body, outs, [spots, shares, *parts], [pltpu.VMEM((SLOTS, width), BF16)], flops)


def shards(
    query_heads,
    key_heads,
    value_heads,
    out_weight,
    norm_gain,
    gate_up_weight,
    down_weight,
    expert_ids,
    route_weights,
):
    tok_rows = query_heads.shape[0]
    device_index = lax.axis_index("ep")
    z, y, c = device_index // (NY * NC), device_index // NC % NY, device_index % NC
    first_pos = device_index * tok_rows

    def plan_of(ids, weights):
        coarse = lax.reduce_precision(weights, 8, 7)
        fine = lax.reduce_precision(weights - coarse, 8, 7)
        lanes = [
            jnp.concatenate([ids.astype(F32).T, ranks_of(ids).T], 0),
            jnp.concatenate([coarse.T, fine.T], 0),
        ]
        plan = jnp.concatenate([*lanes, jnp.zeros_like(lanes[0])], 1).astype(BF16)
        return jnp.concatenate([plan, jnp.zeros_like(plan)], 0)

    def before_of(keys, values):
        before = from_behind((keys, values), 1)
        return [jnp.concatenate(pair, 0) for pair in zip(before, (keys, values))]

    def attend(queries, keys, values):
        return window_attention(queries, keys, values, first_pos, first_pos - WIN)

    x = lax.axis_index("dp")
    quarters, spots, shares = projection(
        (attend, query_heads),
        (before_of, (key_heads, value_heads)),
        (plan_of, (expert_ids, route_weights)),
        out_weight,
        x,
        z,
        y,
        c,
    )
    hidden, normed = join_and_norm(quarters, norm_gain, x)

    near_count, half = len(GROUPS[0]), tok_rows // 2
    near_spots, far_spots = spots[:near_count], spots[near_count:]
    every = range(len(WAYS))

    def spread(rows, lots, back=False):
        sign = -1 if back else 1
        return {i: moved(rows[i], dy=sign * WAYS[i][0], flip=WAYS[i][1]) for i in lots}

    same_plane = [[index_of(i, j, k) for j in range(NY) for k in range(NC)] for i in range(NZ)]

    def exchange(rows):
        rows = rows.reshape(NY * NC, -1, rows.shape[1])
        rows = lax.all_to_all(
            rows, "ep", split_axis=0, concat_axis=0, tiled=True, axis_index_groups=same_plane
        )
        return rows.reshape(-1, rows.shape[2])

    up, down = moved(normed, dz=1), moved(normed, dz=-1)
    held = [normed, down, up]
    up, down = moved(up, dz=1), moved(down, dz=-1)
    [rows] = pick_rows(near_spots, [*held, down, up], joined=True)
    up, down, rows = tied((up, down, rows))
    got = exchange(rows)
    up, down = moved(up, dz=1), moved(down, dz=-1)
    held = [down, up]
    low, high = moved(up[:half], dz=1), moved(down[half:], dz=-1)
    far_rows = pick_rows(far_spots, [*held, (low, high)])
    far_got = spread(far_rows, every)
    [made] = run_expert([got], gate_up_weight[0], down_weight[0])
    far_got, made = tied((far_got, made))
    far_made = run_expert([far_got[i] for i in every], gate_up_weight[0], down_weight[0])
    far_back = spread(far_made, every, back=True)
    sums = combine(far_spots, shares[near_count:], [far_back[i] for i in every], len(GROUPS[1]))
    partial = dict(zip(GROUPS[1], sums))
    *far_made, made = tied((*far_made, made))
    back = exchange(made)
    up = moved(partial[4][half:].astype(BF16), dz=1)
    down = moved(partial[4][:half].astype(BF16), dz=-1)
    up = partial[3] + jnp.pad(up.astype(F32), ((half, 0), (0, 0)))
    down = partial[-3] + jnp.pad(down.astype(F32), ((0, half), (0, 0)))
    up, down = moved(up.astype(BF16), dz=1), moved(down.astype(BF16), dz=-1)
    sums = combine(near_spots, shares[:near_count], [back], near_count)
    partial.update(zip(GROUPS[0], sums))
    up, down = up.astype(F32) + partial[2], down.astype(F32) + partial[-2]
    for step in (1, 0):
        up = moved(up.astype(BF16), dz=1).astype(F32)
        down = moved(down.astype(BF16), dz=-1).astype(F32)
        if step:
            up, down = up + partial[step], down + partial[-step]
    return (hidden.astype(F32) + (partial[0] + up + down)).astype(BF16)


def solution(mesh):
    placed = (
        P(("dp", "ep"), None),
        P(("dp", "ep"), None),
        P(("dp", "ep"), None),
        P("ep", None),
        P(),
        P("ep", None, None),
        P("ep", None, None),
        P(("dp", "ep"), None),
        P(("dp", "ep"), None),
    )
    return jax.shard_map(
        shards, mesh=mesh, in_specs=placed, out_specs=P(("dp", "ep"), None), check_vma=False
    )
```

```python
import jax
import jax.numpy as jnp
from jax import lax
from jax.experimental import pallas as pl
from jax.experimental.pallas import tpu as pltpu
from jax.sharding import PartitionSpec as P

HD = 64
WIN = 128
NX, NZ, NY, NC = 4, 8, 4, 2
CAP = 16
QUARTER = 384
SLOTS = NY * NC * CAP
GROUPS = ((0, 1, -1, 2, -2), (3, -3, 4))
WAYS = tuple((dy, flip) for dy in range(NY) for flip in range(NC))
TOP = 4
BF16 = jnp.bfloat16
F32 = jnp.float32


def tied(values):
    return lax.optimization_barrier(values)


def index_of(z, y, c):
    return ((z % NZ) * NY + y % NY) * NC + c


def moved(block, dz=0, dy=0, flip=False):
    if not (dz or dy or flip):
        return block
    route = [
        (index_of(z, y, c), index_of(z + dz, y + dy, 1 - c if flip else c))
        for z in range(NZ)
        for y in range(NY)
        for c in range(NC)
    ]
    return lax.ppermute(block, "ep", route)


def from_behind(block, distance):
    devices = range(NZ * NY * NC)
    route = [(i - distance, i) for i in devices if i - distance in devices]
    return lax.ppermute(block, "ep", route)


def window_attention(queries, before, here, first_pos):
    rows, width = queries.shape
    heads_width = here[0].shape[1]
    group = width // heads_width
    lanes = 2 * HD

    def body(first_ref, query_ref, *refs):
        *ins, out_ref, keys, values = refs
        for i, to in ((0, keys), (1, values)):
            to[:rows, :], to[rows:, :] = ins[i][...], ins[2 + i][...]
        row = lax.broadcasted_iota(jnp.int32, (rows, 2 * rows), 0)
        key = lax.broadcasted_iota(jnp.int32, (rows, 2 * rows), 1)
        distance = row + rows - key
        allowed = (distance >= 0) & (distance < WIN) & (first_ref[0] - rows + key >= 0)
        half = lax.broadcasted_iota(jnp.int32, (2 * rows, lanes), 1) // HD
        for g in range(heads_width // HD):
            sides = []
            for ref in (keys, values):
                pair = ref[:, g // 2 * lanes : (g // 2 + 1) * lanes].astype(F32)
                alone = jnp.where(half == g % 2, pair, 0.0)
                both = [alone.astype(BF16), pltpu.roll(alone, HD, 1).astype(BF16)]
                sides.append(both if g % 2 == 0 else both[::-1])
            for p in range(group // 2):
                first = g * group * HD + p * lanes
                query = query_ref[:, first : first + lanes]
                mixed = 0.0
                for key_side, value_side in zip(*sides):
                    scores = lax.dot_general(
                        query, key_side, (((1,), (1,)), ((), ())), preferred_element_type=F32
                    ) * HD ** (-0.5)
                    scores = jnp.where(allowed, scores, -1e30)
                    exp_scores = jnp.exp(scores - jnp.max(scores, axis=-1, keepdims=True))
                    whole = jnp.sum(exp_scores, axis=-1, keepdims=True)
                    probs = (exp_scores / whole).astype(BF16)
                    mixed += jnp.dot(probs, value_side, preferred_element_type=F32)
                out_ref[:, first : first + lanes] = mixed.astype(BF16)

    outs = [jax.ShapeDtypeStruct((rows, width), BF16)]
    scratch = [pltpu.VMEM((2 * rows, heads_width), BF16)] * 2
    args = [first_pos.reshape(1), queries, *before, *here]
    return call(body, outs, args, scratch, 8 * rows * rows * width, scalars=1)[0]


def moved_x(block, dx):
    return lax.ppermute(block, "dp", [(x, (x + dx) % NX) for x in range(NX)])


def in_order(pieces, first, count):
    return lax.dynamic_slice_in_dim(jnp.stack(pieces + pieces), (count - first) % count, count, 0)


def projection(attend, before_of, plan_of, out_weight, x, z, y, c):
    depth, width = out_weight.shape
    padded = jnp.pad(out_weight, ((0, 0), (0, NX * QUARTER - width)))
    kept = lax.dynamic_slice_in_dim(padded, x * QUARTER, QUARTER, 1)
    (attend, queries), (before_of, before), (plan_of, plan) = attend, before_of, plan_of
    swapped, before, plan = tied((moved(kept, flip=True), before, plan))
    plan, span = plan_of(*plan), before_of(*before)
    chip = in_order([kept, swapped], c, NC).reshape(-1, QUARTER)
    around = [chip, moved(chip, dy=-1), moved(chip, dy=2), moved(chip, dy=1)]
    plane = in_order(around, y, NY).reshape(-1, QUARTER)
    taken = plane.shape[0]
    plane, queries = tied((jnp.concatenate([plane, plan], 0), queries))
    split = plane.shape[0] // 2 // 16 * 16
    up, down, context = tied(
        (moved(plane, dz=1), moved(plane, dz=-1), attend(queries, *span))
    )
    parts = {0: plane, -1: up, 1: down}
    for step in (2, 3):
        up, down = moved(up, dz=1), moved(down, dz=-1)
        parts[-step], parts[step] = up, down
    parts[4] = (moved(up[:split], dz=1), moved(down[split:], dz=-1))
    rows = context.shape[0]
    up, down = moved_x(context, 1), moved_x(context, -1)
    low, high = moved_x(up[: rows // 2], 1), moved_x(down[rows // 2 :], -1)
    *quarters, spots, shares = multiply(parts, [context, down, low, high, up], (z, y, c))
    quarters = [
        quarters[0],
        moved_x(quarters[3], -1),
        moved_x(quarters[2], 2),
        moved_x(quarters[1], 1),
    ]
    return quarters, spots, shares


def multiply(parts, contexts, place):
    order = [d for group in GROUPS for d in group]
    pieces = [parts[d] if isinstance(parts[d], tuple) else (parts[d],) for d in order]
    flat = [piece for b in pieces for piece in b]
    taken, depth = parts[0].shape[0], contexts[0].shape[1]
    share = depth // NZ
    rows = contexts[0].shape[0]
    tall = sum(b.shape[0] for b in contexts)

    def body(place_ref, *refs):
        weights, ins = refs[: len(flat)], refs[len(flat) : len(flat) + len(contexts)]
        *outs, spots_ref, shares_ref, whole, joined = refs[len(flat) + len(contexts) :]
        z, y, c = place_ref[0], place_ref[1], place_ref[2]
        first = 0
        for piece in ins:
            whole[first : first + piece.shape[0], :] = piece[...]
            first += piece.shape[0]
        total = jnp.zeros((tall, QUARTER), F32)
        at = 0
        for k, d in enumerate(order):
            part = weights[at]
            if len(pieces[k]) > 1:
                first = 0
                for piece in pieces[k]:
                    joined[first : first + piece.shape[0], :] = weights[at][...]
                    first, at = first + piece.shape[0], at + 1
                part = joined
            else:
                at += 1
            column = pl.multiple_of(lax.rem(z + (d + NZ), NZ) * share, share)
            total += jnp.dot(
                whole[:, pl.ds(column, share)], part[:share, :], preferred_element_type=F32
            )
            plan = part[share : share + 2 * TOP, :].astype(F32)
            expert = plan[:TOP, :rows].astype(jnp.int32) - z * (NY * NC)
            rank = plan[TOP:, :rows].astype(jnp.int32)
            way = expert
            if k >= len(GROUPS[0]):
                way = (((expert >> 1) - y) & (NY - 1)) * NC + ((expert & 1) ^ c)
            here = (expert >= 0) & (expert < NY * NC)
            spots_ref[k] = jnp.where(here, way * CAP + rank, -1)
            shares_ref[k] = plan[:, rows : 2 * rows]
        total = total.astype(BF16)
        for k, out in enumerate(outs):
            out[...] = total[k * rows : (k + 1) * rows]

    outs = [jax.ShapeDtypeStruct((rows, QUARTER), BF16)] * NX
    outs.append(jax.ShapeDtypeStruct((NZ, TOP, rows), jnp.int32))
    outs.append(jax.ShapeDtypeStruct((NZ, 2 * TOP, rows), F32))
    scratch = [pltpu.VMEM((tall, depth), BF16), pltpu.VMEM((taken, QUARTER), BF16)]
    args = [jnp.stack(place), *flat, *contexts]
    return call(body, outs, args, scratch, 2 * tall * depth * QUARTER, scalars=1)


def join_and_norm(quarters, gain, x):
    rows, width = quarters[0].shape[0], gain.shape[0]

    def body(x_ref, gain_ref, *refs):
        ins, (hidden_ref, normed_ref, whole) = refs[:NX], refs[NX:]
        for k, piece in enumerate(ins):
            first = pl.multiple_of((x_ref[0] + k) % NX * QUARTER, QUARTER)
            whole[:, pl.ds(first, QUARTER)] = piece[...]
        hidden = whole[:, :width]
        hidden_ref[...] = hidden
        hidden = hidden.astype(F32)
        scale = lax.rsqrt(jnp.mean(hidden * hidden, axis=-1, keepdims=True) + 1e-05)
        normed_ref[...] = (hidden * scale * gain_ref[...]).astype(BF16)

    in_vmem = pl.BlockSpec(memory_space=pltpu.VMEM)
    return pl.pallas_call(
        body,
        out_shape=(jax.ShapeDtypeStruct((rows, width), BF16),) * 2,
        in_specs=[pl.BlockSpec(memory_space=pltpu.SMEM)] + [in_vmem] * (NX + 1),
        out_specs=(in_vmem,) * 2,
        scratch_shapes=[pltpu.VMEM((rows, NX * QUARTER), BF16)],
        compiler_params=pltpu.CompilerParams(vmem_limit_bytes=16 << 20),
    )(x.reshape(1), gain.reshape(1, -1), *quarters)


def ranks_of(expert_ids):
    rows = expert_ids.shape[0]
    experts = jnp.arange(NZ * NY * NC, dtype=jnp.int32)
    named = expert_ids[:, :, None] == experts
    marks = jnp.sum(named.astype(F32), axis=1).astype(BF16)
    steps = jnp.arange(rows)
    earlier = (steps[:, None] > steps[None, :]).astype(BF16)
    counts = jnp.dot(earlier, marks, preferred_element_type=F32)
    return jnp.sum(jnp.where(named, counts[:, None, :], 0.0), axis=2)


def call(body, outs, args, scratch=(), flops=0, limit=40, scalars=0):
    moved_bytes = sum(a.size * a.dtype.itemsize for a in (*args, *outs))
    return pl.pallas_call(
        body,
        out_shape=tuple(outs),
        in_specs=[pl.BlockSpec(memory_space=pltpu.SMEM)] * scalars
        + [pl.BlockSpec(memory_space=pltpu.VMEM)] * (len(args) - scalars),
        out_specs=tuple(pl.BlockSpec(memory_space=pltpu.VMEM) for _ in outs),
        scratch_shapes=list(scratch),
        compiler_params=pltpu.CompilerParams(vmem_limit_bytes=limit << 20),
        cost_estimate=pl.CostEstimate(
            flops=flops, bytes_accessed=moved_bytes, transcendentals=0
        ),
    )(*args)


def pick_rows(spots, base, blocks, joined=False):
    pieces = [b if isinstance(b, tuple) else (b,) for b in blocks]
    flat = [piece for b in pieces for piece in b]
    count, (rows, width) = len(blocks), blocks[0].shape

    def body(spots_ref, *refs):
        ins, outs, whole = refs[: len(flat)], refs[len(flat) : -1], refs[-1]
        slot = lax.broadcasted_iota(jnp.int32, (SLOTS, rows), 0)
        at = 0
        for b in range(count):
            if len(pieces[b]) > 1:
                first = 0
                for piece in pieces[b]:
                    whole[first : first + piece.shape[0], :] = ins[at][...]
                    first, at = first + piece.shape[0], at + 1
                block = whole[...]
            else:
                block, at = ins[at][...], at + 1
            pick = jnp.zeros((SLOTS, rows), F32)
            for r in range(TOP):
                pick += jnp.where(spots_ref[base + b, r : r + 1, :] == slot, 1.0, 0.0)
            found = jnp.dot(pick.astype(BF16), block, preferred_element_type=F32).astype(BF16)
            for i in range(len(WAYS)):
                to, first = (outs[0], i * count * CAP) if joined else (outs[i], 0)
                first += b * CAP
                to[first : first + CAP, :] = found[i * CAP : (i + 1) * CAP]

    outs = [jax.ShapeDtypeStruct((count * CAP, width), BF16)] * len(WAYS)
    if joined:
        outs = [jax.ShapeDtypeStruct((len(WAYS) * count * CAP, width), BF16)]
    flops = 2 * count * SLOTS * rows * width
    return call(body, outs, [spots, *flat], [pltpu.VMEM((rows, width), BF16)], flops)


def run_expert(parts, gate_up, down):
    rows, width = parts[0].shape
    total, units = rows * len(parts), down.shape[0]
    wide, tall = 512, 128
    firsts = [(at, min(at + wide, 2 * units)) for at in range(0, 2 * units, wide)]

    def body(gate_up_hbm, down_hbm, *refs):
        ins, outs = refs[: len(parts)], refs[len(parts) : -5]
        taken, projected, gate_up_ref, down_ref, sems = refs[-5:]
        copies = [
            pltpu.make_async_copy(
                gate_up_hbm.at[:, first:last], gate_up_ref.at[:, first:last], sems.at[i]
            )
            for i, (first, last) in enumerate(firsts)
        ]
        copies.append(pltpu.make_async_copy(down_hbm, down_ref, sems.at[len(firsts)]))
        for copy in copies:
            copy.start()
        for i, part in enumerate(ins):
            taken[i * rows : (i + 1) * rows, :] = part[...]
        for copy, (first, last) in zip(copies, firsts):
            copy.wait()
            projected[:, first:last] = jnp.dot(
                taken[...], gate_up_ref[:, first:last], preferred_element_type=F32
            )
        for first in range(0, total, tall):
            gate = projected[first : first + tall, :units]
            up = projected[first : first + tall, units:]
            active = (up + 1.0) * gate * jax.nn.sigmoid(1.702 * gate)
            taken[first : first + tall, :] = active.astype(BF16)
        copies[-1].wait()
        for first in range(0, width, wide):
            last = min(first + wide, width)
            made = jnp.dot(taken[...], down_ref[:, first:last], preferred_element_type=F32)
            made = made.astype(BF16)
            for i, out in enumerate(outs):
                out[:, first:last] = made[i * rows : (i + 1) * rows]

    in_vmem = pl.BlockSpec(memory_space=pltpu.VMEM)
    anywhere = pl.BlockSpec(memory_space=pl.ANY)
    return pl.pallas_call(
        body,
        out_shape=tuple([jax.ShapeDtypeStruct((rows, width), BF16)] * len(parts)),
        in_specs=[anywhere] * 2 + [in_vmem] * len(parts),
        out_specs=(in_vmem,) * len(parts),
        scratch_shapes=[
            pltpu.VMEM((total, width), BF16),
            pltpu.VMEM((total, 2 * units), F32),
            pltpu.VMEM(gate_up.shape, BF16),
            pltpu.VMEM(down.shape, BF16),
            pltpu.SemaphoreType.DMA((len(firsts) + 1,)),
        ],
        compiler_params=pltpu.CompilerParams(vmem_limit_bytes=40 << 20),
        cost_estimate=pl.CostEstimate(
            flops=6 * total * width * units,
            bytes_accessed=6 * width * units + 4 * total * width,
            transcendentals=0,
        ),
    )(gate_up, down, *parts)


def combine(spots, shares, base, parts, count):
    width = parts[0].shape[1]
    rows = spots.shape[2]

    def body(spots_ref, shares_ref, *refs):
        ins, outs, whole = refs[: len(parts)], refs[len(parts) : -1], refs[-1]
        slot = lax.broadcasted_iota(jnp.int32, (SLOTS, rows), 0)
        for b in range(count):
            for i in range(len(WAYS)):
                part, first = (ins[i], 0) if len(parts) > 1 else (ins[0], i * count * CAP)
                first += b * CAP
                whole[i * CAP : (i + 1) * CAP, :] = part[first : first + CAP, :]
            sums = 0.0
            for fine in range(2):
                share = jnp.zeros((SLOTS, rows), F32)
                for r in range(TOP):
                    here = spots_ref[base + b, r : r + 1, :] == slot
                    at = fine * TOP + r
                    share += jnp.where(here, shares_ref[base + b, at : at + 1, :], 0.0)
                sums += jnp.dot(share.T.astype(BF16), whole[...], preferred_element_type=F32)
            outs[b][...] = sums

    outs = [jax.ShapeDtypeStruct((rows, width), F32)] * count
    flops = 4 * count * SLOTS * rows * width
    return call(body, outs, [spots, shares, *parts], [pltpu.VMEM((SLOTS, width), BF16)], flops)


def shards(
    query_heads,
    key_heads,
    value_heads,
    out_weight,
    norm_gain,
    gate_up_weight,
    down_weight,
    expert_ids,
    route_weights,
):
    tok_rows = query_heads.shape[0]
    device_index = lax.axis_index("ep")
    z, y, c = device_index // (NY * NC), device_index // NC % NY, device_index % NC
    first_pos = device_index * tok_rows

    def plan_of(ids, weights):
        coarse = lax.reduce_precision(weights, 8, 7)
        fine = lax.reduce_precision(weights - coarse, 8, 7)
        lanes = [
            jnp.concatenate([ids.astype(F32).T, ranks_of(ids).T], 0),
            jnp.concatenate([coarse.T, fine.T], 0),
        ]
        plan = jnp.concatenate([*lanes, jnp.zeros_like(lanes[0])], 1).astype(BF16)
        return jnp.concatenate([plan, jnp.zeros_like(plan)], 0)

    def before_of(keys, values):
        return from_behind((keys, values), 1), (keys, values)

    def attend(queries, before, here):
        return window_attention(queries, before, here, first_pos)

    x = lax.axis_index("dp")
    quarters, spots, shares = projection(
        (attend, query_heads),
        (before_of, (key_heads, value_heads)),
        (plan_of, (expert_ids, route_weights)),
        out_weight,
        x,
        z,
        y,
        c,
    )
    hidden, normed = join_and_norm(quarters, norm_gain, x)

    near_count, half = len(GROUPS[0]), tok_rows // 2
    every = range(len(WAYS))

    def spread(rows, lots, back=False):
        sign = -1 if back else 1
        return {i: moved(rows[i], dy=sign * WAYS[i][0], flip=WAYS[i][1]) for i in lots}

    same_plane = [[index_of(i, j, k) for j in range(NY) for k in range(NC)] for i in range(NZ)]

    def exchange(rows):
        rows = rows.reshape(NY * NC, -1, rows.shape[1])
        rows = lax.all_to_all(
            rows, "ep", split_axis=0, concat_axis=0, tiled=True, axis_index_groups=same_plane
        )
        return rows.reshape(-1, rows.shape[2])

    up, down = moved(normed, dz=1), moved(normed, dz=-1)
    held = [normed, down, up]
    up, down = moved(up, dz=1), moved(down, dz=-1)
    [rows] = pick_rows(spots, 0, [*held, down, up], joined=True)
    up, down, rows = tied((up, down, rows))
    got = exchange(rows)
    up, down = moved(up, dz=1), moved(down, dz=-1)
    held = [down, up]
    low, high = moved(up[:half], dz=1), moved(down[half:], dz=-1)
    far_rows = pick_rows(spots, near_count, [*held, (low, high)])
    far_got = spread(far_rows, every)
    far_made = run_expert([far_got[i] for i in every], gate_up_weight[0], down_weight[0])
    far_made, got = tied((far_made, got))
    far_back = spread(far_made, every, back=True)
    [made] = run_expert([got], gate_up_weight[0], down_weight[0])
    sums = combine(spots, shares, near_count, [far_back[i] for i in every], len(GROUPS[1]))
    partial = dict(zip(GROUPS[1], sums))
    back = exchange(made)
    up = moved(partial[4][half:].astype(BF16), dz=1)
    down = moved(partial[4][:half].astype(BF16), dz=-1)
    up = partial[3] + jnp.pad(up.astype(F32), ((half, 0), (0, 0)))
    down = partial[-3] + jnp.pad(down.astype(F32), ((0, half), (0, 0)))
    up, down = moved(up.astype(BF16), dz=1), moved(down.astype(BF16), dz=-1)
    sums = combine(spots, shares, 0, [back], near_count)
    partial.update(zip(GROUPS[0], sums))
    up, down = up.astype(F32) + partial[2], down.astype(F32) + partial[-2]
    for step in (1, 0):
        up = moved(up.astype(BF16), dz=1).astype(F32)
        down = moved(down.astype(BF16), dz=-1).astype(F32)
        if step:
            up, down = up + partial[step], down + partial[-step]
    return (hidden.astype(F32) + (partial[0] + up + down)).astype(BF16)


def solution(mesh):
    placed = (
        P(("dp", "ep"), None),
        P(("dp", "ep"), None),
        P(("dp", "ep"), None),
        P("ep", None),
        P(),
        P("ep", None, None),
        P("ep", None, None),
        P(("dp", "ep"), None),
        P(("dp", "ep"), None),
    )
    return jax.shard_map(
        shards, mesh=mesh, in_specs=placed, out_specs=P(("dp", "ep"), None), check_vma=False
    )
```

```python
import jax
import jax.numpy as jnp
from jax import lax
from jax.experimental import pallas as pl
from jax.experimental.pallas import tpu as pltpu
from jax.sharding import PartitionSpec as P

HD = 64
WIN = 128
NX, NZ, NY, NC = 4, 8, 4, 2
CAP = 16
QUARTER = 384
SLOTS = NY * NC * CAP
GROUPS = ((0, 1, -1, 2, -2), (3, -3, 4))
WAYS = tuple((dy, flip) for dy in range(NY) for flip in range(NC))
TOP = 4
BF16 = jnp.bfloat16
F32 = jnp.float32


def tied(values):
    return lax.optimization_barrier(values)


def index_of(z, y, c):
    return ((z % NZ) * NY + y % NY) * NC + c


def moved(block, dz=0, dy=0, flip=False):
    if not (dz or dy or flip):
        return block
    route = [
        (index_of(z, y, c), index_of(z + dz, y + dy, 1 - c if flip else c))
        for z in range(NZ)
        for y in range(NY)
        for c in range(NC)
    ]
    return lax.ppermute(block, "ep", route)


def from_behind(block, distance):
    devices = range(NZ * NY * NC)
    route = [(i - distance, i) for i in devices if i - distance in devices]
    return lax.ppermute(block, "ep", route)


def window_attention(queries, before, here, first_pos):
    rows, width = queries.shape
    heads_width = here[0].shape[1]
    group = width // heads_width
    lanes = 2 * HD

    def body(first_ref, query_ref, *refs):
        *ins, out_ref, keys, values = refs
        for i, to in ((0, keys), (1, values)):
            to[:rows, :], to[rows:, :] = ins[i][...], ins[2 + i][...]
        row = lax.broadcasted_iota(jnp.int32, (rows, 2 * rows), 0)
        key = lax.broadcasted_iota(jnp.int32, (rows, 2 * rows), 1)
        distance = row + rows - key
        allowed = (distance >= 0) & (distance < WIN) & (first_ref[0] - rows + key >= 0)
        half = lax.broadcasted_iota(jnp.int32, (2 * rows, lanes), 1) // HD
        for g in range(heads_width // HD):
            sides = []
            for ref in (keys, values):
                pair = ref[:, g // 2 * lanes : (g // 2 + 1) * lanes].astype(F32)
                alone = jnp.where(half == g % 2, pair, 0.0)
                both = [alone.astype(BF16), pltpu.roll(alone, HD, 1).astype(BF16)]
                sides.append(both if g % 2 == 0 else both[::-1])
            for p in range(group // 2):
                first = g * group * HD + p * lanes
                query = query_ref[:, first : first + lanes]
                mixed = 0.0
                for key_side, value_side in zip(*sides):
                    scores = lax.dot_general(
                        query, key_side, (((1,), (1,)), ((), ())), preferred_element_type=F32
                    ) * HD ** (-0.5)
                    scores = jnp.where(allowed, scores, -1e30)
                    exp_scores = jnp.exp(scores - jnp.max(scores, axis=-1, keepdims=True))
                    whole = jnp.sum(exp_scores, axis=-1, keepdims=True)
                    probs = (exp_scores / whole).astype(BF16)
                    mixed += jnp.dot(probs, value_side, preferred_element_type=F32)
                out_ref[:, first : first + lanes] = mixed.astype(BF16)

    outs = [jax.ShapeDtypeStruct((rows, width), BF16)]
    scratch = [pltpu.VMEM((2 * rows, heads_width), BF16)] * 2
    args = [first_pos.reshape(1), queries, *before, *here]
    return call(body, outs, args, scratch, 80 * rows * rows * width, scalars=1)[0]


def moved_x(block, dx):
    return lax.ppermute(block, "dp", [(x, (x + dx) % NX) for x in range(NX)])


def in_order(pieces, first, count):
    return lax.dynamic_slice_in_dim(jnp.stack(pieces + pieces), (count - first) % count, count, 0)


def projection(attend, before_of, plan_of, out_weight, x, z, y, c):
    depth, width = out_weight.shape
    padded = jnp.pad(out_weight, ((0, 0), (0, NX * QUARTER - width)))
    kept = lax.dynamic_slice_in_dim(padded, x * QUARTER, QUARTER, 1)
    (attend, queries), (before_of, before), (plan_of, plan) = attend, before_of, plan_of
    swapped, before, plan = tied((moved(kept, flip=True), before, plan))
    plan, span = plan_of(*plan), before_of(*before)
    chip = in_order([kept, swapped], c, NC).reshape(-1, QUARTER)
    around = [chip, moved(chip, dy=-1), moved(chip, dy=2), moved(chip, dy=1)]
    plane = in_order(around, y, NY).reshape(-1, QUARTER)
    taken = plane.shape[0]
    plane, queries = tied((jnp.concatenate([plane, plan], 0), queries))
    split = plane.shape[0] // 2 // 16 * 16
    up, down, context = tied(
        (moved(plane, dz=1), moved(plane, dz=-1), attend(queries, *span))
    )
    parts = {0: plane, -1: up, 1: down}
    for step in (2, 3):
        up, down = moved(up, dz=1), moved(down, dz=-1)
        parts[-step], parts[step] = up, down
    parts[4] = (moved(up[:split], dz=1), moved(down[split:], dz=-1))
    rows = context.shape[0]
    up, down = moved_x(context, 1), moved_x(context, -1)
    low, high = moved_x(up[: rows // 2], 1), moved_x(down[rows // 2 :], -1)
    *quarters, spots, shares = multiply(parts, [context, down, low, high, up], (z, y, c))
    quarters = [
        quarters[0],
        moved_x(quarters[3], -1),
        moved_x(quarters[2], 2),
        moved_x(quarters[1], 1),
    ]
    return quarters, spots, shares


def multiply(parts, contexts, place):
    order = [d for group in GROUPS for d in group]
    pieces = [parts[d] if isinstance(parts[d], tuple) else (parts[d],) for d in order]
    flat = [piece for b in pieces for piece in b]
    taken, depth = parts[0].shape[0], contexts[0].shape[1]
    share = depth // NZ
    rows = contexts[0].shape[0]
    tall = sum(b.shape[0] for b in contexts)

    def body(place_ref, *refs):
        weights, ins = refs[: len(flat)], refs[len(flat) : len(flat) + len(contexts)]
        *outs, spots_ref, shares_ref, whole, joined = refs[len(flat) + len(contexts) :]
        z, y, c = place_ref[0], place_ref[1], place_ref[2]
        first = 0
        for piece in ins:
            whole[first : first + piece.shape[0], :] = piece[...]
            first += piece.shape[0]
        total = jnp.zeros((tall, QUARTER), F32)
        at = 0
        for k, d in enumerate(order):
            part = weights[at]
            if len(pieces[k]) > 1:
                first = 0
                for piece in pieces[k]:
                    joined[first : first + piece.shape[0], :] = weights[at][...]
                    first, at = first + piece.shape[0], at + 1
                part = joined
            else:
                at += 1
            column = pl.multiple_of(lax.rem(z + (d + NZ), NZ) * share, share)
            total += jnp.dot(
                whole[:, pl.ds(column, share)], part[:share, :], preferred_element_type=F32
            )
            plan = part[share : share + 2 * TOP, :].astype(F32)
            expert = plan[:TOP, :rows].astype(jnp.int32) - z * (NY * NC)
            rank = plan[TOP:, :rows].astype(jnp.int32)
            way = expert
            if k >= len(GROUPS[0]):
                way = (((expert >> 1) - y) & (NY - 1)) * NC + ((expert & 1) ^ c)
            here = (expert >= 0) & (expert < NY * NC)
            spots_ref[k] = jnp.where(here, way * CAP + rank, -1)
            shares_ref[k] = plan[:, rows : 2 * rows]
        total = total.astype(BF16)
        for k, out in enumerate(outs):
            out[...] = total[k * rows : (k + 1) * rows]

    outs = [jax.ShapeDtypeStruct((rows, QUARTER), BF16)] * NX
    outs.append(jax.ShapeDtypeStruct((NZ, TOP, rows), jnp.int32))
    outs.append(jax.ShapeDtypeStruct((NZ, 2 * TOP, rows), F32))
    scratch = [pltpu.VMEM((tall, depth), BF16), pltpu.VMEM((taken, QUARTER), BF16)]
    args = [jnp.stack(place), *flat, *contexts]
    return call(body, outs, args, scratch, 2 * tall * depth * QUARTER, scalars=1)


def join_and_norm(quarters, gain, x):
    rows, width = quarters[0].shape[0], gain.shape[0]

    def body(x_ref, gain_ref, *refs):
        ins, (hidden_ref, normed_ref, whole) = refs[:NX], refs[NX:]
        for k, piece in enumerate(ins):
            first = pl.multiple_of((x_ref[0] + k) % NX * QUARTER, QUARTER)
            whole[:, pl.ds(first, QUARTER)] = piece[...]
        hidden = whole[:, :width]
        hidden_ref[...] = hidden
        hidden = hidden.astype(F32)
        scale = lax.rsqrt(jnp.mean(hidden * hidden, axis=-1, keepdims=True) + 1e-05)
        normed_ref[...] = (hidden * scale * gain_ref[...]).astype(BF16)

    in_vmem = pl.BlockSpec(memory_space=pltpu.VMEM)
    return pl.pallas_call(
        body,
        out_shape=(jax.ShapeDtypeStruct((rows, width), BF16),) * 2,
        in_specs=[pl.BlockSpec(memory_space=pltpu.SMEM)] + [in_vmem] * (NX + 1),
        out_specs=(in_vmem,) * 2,
        scratch_shapes=[pltpu.VMEM((rows, NX * QUARTER), BF16)],
        compiler_params=pltpu.CompilerParams(vmem_limit_bytes=16 << 20),
    )(x.reshape(1), gain.reshape(1, -1), *quarters)


def ranks_of(expert_ids):
    rows = expert_ids.shape[0]
    experts = jnp.arange(NZ * NY * NC, dtype=jnp.int32)
    named = expert_ids[:, :, None] == experts
    marks = jnp.sum(named.astype(F32), axis=1).astype(BF16)
    steps = jnp.arange(rows)
    earlier = (steps[:, None] > steps[None, :]).astype(BF16)
    counts = jnp.dot(earlier, marks, preferred_element_type=F32)
    return jnp.sum(jnp.where(named, counts[:, None, :], 0.0), axis=2)


def call(body, outs, args, scratch=(), flops=0, limit=40, scalars=0):
    moved_bytes = sum(a.size * a.dtype.itemsize for a in (*args, *outs))
    return pl.pallas_call(
        body,
        out_shape=tuple(outs),
        in_specs=[pl.BlockSpec(memory_space=pltpu.SMEM)] * scalars
        + [pl.BlockSpec(memory_space=pltpu.VMEM)] * (len(args) - scalars),
        out_specs=tuple(pl.BlockSpec(memory_space=pltpu.VMEM) for _ in outs),
        scratch_shapes=list(scratch),
        compiler_params=pltpu.CompilerParams(vmem_limit_bytes=limit << 20),
        cost_estimate=pl.CostEstimate(
            flops=flops, bytes_accessed=moved_bytes, transcendentals=0
        ),
    )(*args)


def pick_rows(spots, base, blocks, joined=False):
    pieces = [b if isinstance(b, tuple) else (b,) for b in blocks]
    flat = [piece for b in pieces for piece in b]
    count, (rows, width) = len(blocks), blocks[0].shape

    def body(spots_ref, *refs):
        ins, outs, whole = refs[: len(flat)], refs[len(flat) : -1], refs[-1]
        slot = lax.broadcasted_iota(jnp.int32, (SLOTS, rows), 0)
        at = 0
        for b in range(count):
            if len(pieces[b]) > 1:
                first = 0
                for piece in pieces[b]:
                    whole[first : first + piece.shape[0], :] = ins[at][...]
                    first, at = first + piece.shape[0], at + 1
                block = whole[...]
            else:
                block, at = ins[at][...], at + 1
            pick = jnp.zeros((SLOTS, rows), F32)
            for r in range(TOP):
                pick += jnp.where(spots_ref[base + b, r : r + 1, :] == slot, 1.0, 0.0)
            found = jnp.dot(pick.astype(BF16), block, preferred_element_type=F32).astype(BF16)
            for i in range(len(WAYS)):
                to, first = (outs[0], i * count * CAP) if joined else (outs[i], 0)
                first += b * CAP
                to[first : first + CAP, :] = found[i * CAP : (i + 1) * CAP]

    outs = [jax.ShapeDtypeStruct((count * CAP, width), BF16)] * len(WAYS)
    if joined:
        outs = [jax.ShapeDtypeStruct((len(WAYS) * count * CAP, width), BF16)]
    flops = 2 * count * SLOTS * rows * width
    return call(body, outs, [spots, *flat], [pltpu.VMEM((rows, width), BF16)], flops)


def run_expert(parts, gate_up, down):
    rows, width = parts[0].shape
    total, units = rows * len(parts), down.shape[0]
    wide, tall = 512, 128
    firsts = [(at, min(at + wide, 2 * units)) for at in range(0, 2 * units, wide)]

    def body(gate_up_hbm, down_hbm, *refs):
        ins, outs = refs[: len(parts)], refs[len(parts) : -5]
        taken, projected, gate_up_ref, down_ref, sems = refs[-5:]
        copies = [
            pltpu.make_async_copy(
                gate_up_hbm.at[:, first:last], gate_up_ref.at[:, first:last], sems.at[i]
            )
            for i, (first, last) in enumerate(firsts)
        ]
        copies.append(pltpu.make_async_copy(down_hbm, down_ref, sems.at[len(firsts)]))
        for copy in copies:
            copy.start()
        for i, part in enumerate(ins):
            taken[i * rows : (i + 1) * rows, :] = part[...]
        for copy, (first, last) in zip(copies, firsts):
            copy.wait()
            projected[:, first:last] = jnp.dot(
                taken[...], gate_up_ref[:, first:last], preferred_element_type=F32
            )
        for first in range(0, total, tall):
            gate = projected[first : first + tall, :units]
            up = projected[first : first + tall, units:]
            active = (up + 1.0) * gate * jax.nn.sigmoid(1.702 * gate)
            taken[first : first + tall, :] = active.astype(BF16)
        copies[-1].wait()
        for first in range(0, width, wide):
            last = min(first + wide, width)
            made = jnp.dot(taken[...], down_ref[:, first:last], preferred_element_type=F32)
            made = made.astype(BF16)
            for i, out in enumerate(outs):
                out[:, first:last] = made[i * rows : (i + 1) * rows]

    in_vmem = pl.BlockSpec(memory_space=pltpu.VMEM)
    in_hbm = pl.BlockSpec(memory_space=pltpu.HBM)
    return pl.pallas_call(
        body,
        out_shape=tuple([jax.ShapeDtypeStruct((rows, width), BF16)] * len(parts)),
        in_specs=[in_hbm] * 2 + [in_vmem] * len(parts),
        out_specs=(in_vmem,) * len(parts),
        scratch_shapes=[
            pltpu.VMEM((total, width), BF16),
            pltpu.VMEM((total, 2 * units), F32),
            pltpu.VMEM(gate_up.shape, BF16),
            pltpu.VMEM(down.shape, BF16),
            pltpu.SemaphoreType.DMA((len(firsts) + 1,)),
        ],
        compiler_params=pltpu.CompilerParams(vmem_limit_bytes=40 << 20),
        cost_estimate=pl.CostEstimate(
            flops=6 * total * width * units,
            bytes_accessed=6 * width * units + 4 * total * width,
            transcendentals=0,
        ),
    )(gate_up, down, *parts)


def combine(spots, shares, base, parts, count):
    width = parts[0].shape[1]
    rows = spots.shape[2]

    def body(spots_ref, shares_ref, *refs):
        ins, outs, whole = refs[: len(parts)], refs[len(parts) : -1], refs[-1]
        slot = lax.broadcasted_iota(jnp.int32, (SLOTS, rows), 0)
        for b in range(count):
            for i in range(len(WAYS)):
                part, first = (ins[i], 0) if len(parts) > 1 else (ins[0], i * count * CAP)
                first += b * CAP
                whole[i * CAP : (i + 1) * CAP, :] = part[first : first + CAP, :]
            sums = 0.0
            for fine in range(2):
                share = jnp.zeros((SLOTS, rows), F32)
                for r in range(TOP):
                    here = spots_ref[base + b, r : r + 1, :] == slot
                    at = fine * TOP + r
                    share += jnp.where(here, shares_ref[base + b, at : at + 1, :], 0.0)
                sums += jnp.dot(share.T.astype(BF16), whole[...], preferred_element_type=F32)
            outs[b][...] = sums

    outs = [jax.ShapeDtypeStruct((rows, width), F32)] * count
    flops = 4 * count * SLOTS * rows * width
    return call(body, outs, [spots, shares, *parts], [pltpu.VMEM((SLOTS, width), BF16)], flops)


def shards(
    query_heads,
    key_heads,
    value_heads,
    out_weight,
    norm_gain,
    gate_up_weight,
    down_weight,
    expert_ids,
    route_weights,
):
    tok_rows = query_heads.shape[0]
    device_index = lax.axis_index("ep")
    z, y, c = device_index // (NY * NC), device_index // NC % NY, device_index % NC
    first_pos = device_index * tok_rows

    def plan_of(ids, weights):
        coarse = lax.reduce_precision(weights, 8, 7)
        fine = lax.reduce_precision(weights - coarse, 8, 7)
        lanes = [
            jnp.concatenate([ids.astype(F32).T, ranks_of(ids).T], 0),
            jnp.concatenate([coarse.T, fine.T], 0),
        ]
        plan = jnp.concatenate([*lanes, jnp.zeros_like(lanes[0])], 1).astype(BF16)
        return jnp.concatenate([plan, jnp.zeros_like(plan)], 0)

    def before_of(keys, values):
        return from_behind((keys, values), 1), (keys, values)

    def attend(queries, before, here):
        return window_attention(queries, before, here, first_pos)

    x = lax.axis_index("dp")
    quarters, spots, shares = projection(
        (attend, query_heads),
        (before_of, (key_heads, value_heads)),
        (plan_of, (expert_ids, route_weights)),
        out_weight,
        x,
        z,
        y,
        c,
    )
    hidden, normed = join_and_norm(quarters, norm_gain, x)

    near_count, half = len(GROUPS[0]), tok_rows // 2
    every = range(len(WAYS))

    def spread(rows, lots, back=False):
        sign = -1 if back else 1
        return {i: moved(rows[i], dy=sign * WAYS[i][0], flip=WAYS[i][1]) for i in lots}

    same_plane = [[index_of(i, j, k) for j in range(NY) for k in range(NC)] for i in range(NZ)]

    def exchange(rows):
        rows = rows.reshape(NY * NC, -1, rows.shape[1])
        rows = lax.all_to_all(
            rows, "ep", split_axis=0, concat_axis=0, tiled=True, axis_index_groups=same_plane
        )
        return rows.reshape(-1, rows.shape[2])

    up, down = moved(normed, dz=1), moved(normed, dz=-1)
    held = [normed, down, up]
    up, down = moved(up, dz=1), moved(down, dz=-1)
    [rows] = pick_rows(spots, 0, [*held, down, up], joined=True)
    up, down, rows = tied((up, down, rows))
    got = exchange(rows)
    up, down = moved(up, dz=1), moved(down, dz=-1)
    held = [down, up]
    low, high = moved(up[:half], dz=1), moved(down[half:], dz=-1)
    far_rows = pick_rows(spots, near_count, [*held, (low, high)])
    far_got = spread(far_rows, every)
    [made] = run_expert([got], gate_up_weight[0], down_weight[0])
    far_got, made = tied((far_got, made))
    far_made = run_expert([far_got[i] for i in every], gate_up_weight[0], down_weight[0])
    far_back = spread(far_made, every, back=True)
    sums = combine(spots, shares, near_count, [far_back[i] for i in every], len(GROUPS[1]))
    partial = dict(zip(GROUPS[1], sums))
    back = exchange(made)
    up = moved(partial[4][half:].astype(BF16), dz=1)
    down = moved(partial[4][:half].astype(BF16), dz=-1)
    up = partial[3] + jnp.pad(up.astype(F32), ((half, 0), (0, 0)))
    down = partial[-3] + jnp.pad(down.astype(F32), ((0, half), (0, 0)))
    up, down = moved(up.astype(BF16), dz=1), moved(down.astype(BF16), dz=-1)
    sums = combine(spots, shares, 0, [back], near_count)
    partial.update(zip(GROUPS[0], sums))
    up, down = up.astype(F32) + partial[2], down.astype(F32) + partial[-2]
    for step in (1, 0):
        up = moved(up.astype(BF16), dz=1).astype(F32)
        down = moved(down.astype(BF16), dz=-1).astype(F32)
        if step:
            up, down = up + partial[step], down + partial[-step]
    return (hidden.astype(F32) + (partial[0] + up + down)).astype(BF16)


def solution(mesh):
    placed = (
        P(("dp", "ep"), None),
        P(("dp", "ep"), None),
        P(("dp", "ep"), None),
        P("ep", None),
        P(),
        P("ep", None, None),
        P("ep", None, None),
        P(("dp", "ep"), None),
        P(("dp", "ep"), None),
    )
    return jax.shard_map(
        shards, mesh=mesh, in_specs=placed, out_specs=P(("dp", "ep"), None), check_vma=False
    )
```

```python
import jax
import jax.numpy as jnp
from jax import lax
from jax.experimental import pallas as pl
from jax.experimental.pallas import tpu as pltpu
from jax.sharding import PartitionSpec as P

HD = 64
WIN = 128
NX, NZ, NY, NC = 4, 8, 4, 2
CAP = 16
QUARTER = 384
SLOTS = NY * NC * CAP
GROUPS = ((0, 1, -1, 2, -2), (3, -3, 4))
WAYS = tuple((dy, flip) for dy in range(NY) for flip in range(NC))
TOP = 4
BF16 = jnp.bfloat16
F32 = jnp.float32


def tied(values):
    return lax.optimization_barrier(values)


def index_of(z, y, c):
    return ((z % NZ) * NY + y % NY) * NC + c


def moved(block, dz=0, dy=0, flip=False):
    if not (dz or dy or flip):
        return block
    route = [
        (index_of(z, y, c), index_of(z + dz, y + dy, 1 - c if flip else c))
        for z in range(NZ)
        for y in range(NY)
        for c in range(NC)
    ]
    return lax.ppermute(block, "ep", route)


def from_behind(block, distance):
    devices = range(NZ * NY * NC)
    route = [(i - distance, i) for i in devices if i - distance in devices]
    return lax.ppermute(block, "ep", route)


def window_attention(queries, before, here, first_pos):
    rows, width = queries.shape
    heads_width = here[0].shape[1]
    group = width // heads_width
    lanes = 2 * HD

    def body(first_ref, query_ref, *refs):
        *ins, out_ref, keys, values = refs
        for i, to in ((0, keys), (1, values)):
            to[:rows, :], to[rows:, :] = ins[i][...], ins[2 + i][...]
        row = lax.broadcasted_iota(jnp.int32, (rows, 2 * rows), 0)
        key = lax.broadcasted_iota(jnp.int32, (rows, 2 * rows), 1)
        distance = row + rows - key
        allowed = (distance >= 0) & (distance < WIN) & (first_ref[0] - rows + key >= 0)
        half = lax.broadcasted_iota(jnp.int32, (2 * rows, lanes), 1) // HD
        for g in range(heads_width // HD):
            sides = []
            for ref in (keys, values):
                pair = ref[:, g // 2 * lanes : (g // 2 + 1) * lanes].astype(F32)
                alone = jnp.where(half == g % 2, pair, 0.0)
                both = [alone.astype(BF16), pltpu.roll(alone, HD, 1).astype(BF16)]
                sides.append(both if g % 2 == 0 else both[::-1])
            for p in range(group // 2):
                first = g * group * HD + p * lanes
                query = query_ref[:, first : first + lanes]
                mixed = 0.0
                for key_side, value_side in zip(*sides):
                    scores = lax.dot_general(
                        query, key_side, (((1,), (1,)), ((), ())), preferred_element_type=F32
                    ) * HD ** (-0.5)
                    scores = jnp.where(allowed, scores, -1e30)
                    exp_scores = jnp.exp(scores - jnp.max(scores, axis=-1, keepdims=True))
                    whole = jnp.sum(exp_scores, axis=-1, keepdims=True)
                    probs = (exp_scores / whole).astype(BF16)
                    mixed += jnp.dot(probs, value_side, preferred_element_type=F32)
                out_ref[:, first : first + lanes] = mixed.astype(BF16)

    outs = [jax.ShapeDtypeStruct((rows, width), BF16)]
    scratch = [pltpu.VMEM((2 * rows, heads_width), BF16)] * 2
    args = [first_pos.reshape(1), queries, *before, *here]
    return call(body, outs, args, scratch, 80 * rows * rows * width, scalars=1)[0]


def moved_x(block, dx):
    return lax.ppermute(block, "dp", [(x, (x + dx) % NX) for x in range(NX)])


def in_order(pieces, first, count):
    return lax.dynamic_slice_in_dim(jnp.stack(pieces + pieces), (count - first) % count, count, 0)


def projection(attend, before_of, plan_of, out_weight, x, z, y, c):
    depth, width = out_weight.shape
    padded = jnp.pad(out_weight, ((0, 0), (0, NX * QUARTER - width)))
    kept = lax.dynamic_slice_in_dim(padded, x * QUARTER, QUARTER, 1)
    (attend, queries), (before_of, before), (plan_of, plan) = attend, before_of, plan_of
    swapped, before, plan = tied((moved(kept, flip=True), before, plan))
    plan, span = plan_of(*plan), before_of(*before)
    chip = in_order([kept, swapped], c, NC).reshape(-1, QUARTER)
    around = [chip, moved(chip, dy=-1), moved(chip, dy=2), moved(chip, dy=1)]
    plane = in_order(around, y, NY).reshape(-1, QUARTER)
    taken = plane.shape[0]
    plane, queries = tied((jnp.concatenate([plane, plan], 0), queries))
    split = plane.shape[0] // 2 // 16 * 16
    up, down, context = tied(
        (moved(plane, dz=1), moved(plane, dz=-1), attend(queries, *span))
    )
    parts = {0: plane, -1: up, 1: down}
    for step in (2, 3):
        up, down = moved(up, dz=1), moved(down, dz=-1)
        parts[-step], parts[step] = up, down
    parts[4] = (moved(up[:split], dz=1), moved(down[split:], dz=-1))
    rows = context.shape[0]
    up, down = moved_x(context, 1), moved_x(context, -1)
    low, high = moved_x(up[: rows // 2], 1), moved_x(down[rows // 2 :], -1)
    *quarters, spots, shares = multiply(parts, [context, down, low, high, up], (z, y, c))
    quarters = [
        quarters[0],
        moved_x(quarters[3], -1),
        moved_x(quarters[2], 2),
        moved_x(quarters[1], 1),
    ]
    return quarters, spots, shares


def multiply(parts, contexts, place):
    order = [d for group in GROUPS for d in group]
    pieces = [parts[d] if isinstance(parts[d], tuple) else (parts[d],) for d in order]
    flat = [piece for b in pieces for piece in b]
    taken, depth = parts[0].shape[0], contexts[0].shape[1]
    share = depth // NZ
    rows = contexts[0].shape[0]
    tall = sum(b.shape[0] for b in contexts)

    def body(place_ref, *refs):
        weights, ins = refs[: len(flat)], refs[len(flat) : len(flat) + len(contexts)]
        *outs, spots_ref, shares_ref, whole, joined = refs[len(flat) + len(contexts) :]
        z, y, c = place_ref[0], place_ref[1], place_ref[2]
        first = 0
        for piece in ins:
            whole[first : first + piece.shape[0], :] = piece[...]
            first += piece.shape[0]
        total = jnp.zeros((tall, QUARTER), F32)
        at = 0
        for k, d in enumerate(order):
            part = weights[at]
            if len(pieces[k]) > 1:
                first = 0
                for piece in pieces[k]:
                    joined[first : first + piece.shape[0], :] = weights[at][...]
                    first, at = first + piece.shape[0], at + 1
                part = joined
            else:
                at += 1
            column = pl.multiple_of(lax.rem(z + (d + NZ), NZ) * share, share)
            total += jnp.dot(
                whole[:, pl.ds(column, share)], part[:share, :], preferred_element_type=F32
            )
            plan = part[share : share + 2 * TOP, :].astype(F32)
            expert = plan[:TOP, :rows].astype(jnp.int32) - z * (NY * NC)
            rank = plan[TOP:, :rows].astype(jnp.int32)
            way = expert
            if k >= len(GROUPS[0]):
                way = (((expert >> 1) - y) & (NY - 1)) * NC + ((expert & 1) ^ c)
            here = (expert >= 0) & (expert < NY * NC)
            spots_ref[k] = jnp.where(here, way * CAP + rank, -1)
            shares_ref[k] = plan[:, rows : 2 * rows]
        total = total.astype(BF16)
        for k, out in enumerate(outs):
            out[...] = total[k * rows : (k + 1) * rows]

    outs = [jax.ShapeDtypeStruct((rows, QUARTER), BF16)] * NX
    outs.append(jax.ShapeDtypeStruct((NZ, TOP, rows), jnp.int32))
    outs.append(jax.ShapeDtypeStruct((NZ, 2 * TOP, rows), F32))
    scratch = [pltpu.VMEM((tall, depth), BF16), pltpu.VMEM((taken, QUARTER), BF16)]
    args = [jnp.stack(place), *flat, *contexts]
    return call(body, outs, args, scratch, 2 * tall * depth * QUARTER, scalars=1)


def join_and_norm(quarters, gain, x):
    rows, width = quarters[0].shape[0], gain.shape[0]

    def body(x_ref, gain_ref, *refs):
        ins, (hidden_ref, normed_ref, whole) = refs[:NX], refs[NX:]
        for k, piece in enumerate(ins):
            first = pl.multiple_of((x_ref[0] + k) % NX * QUARTER, QUARTER)
            whole[:, pl.ds(first, QUARTER)] = piece[...]
        hidden = whole[:, :width]
        hidden_ref[...] = hidden
        hidden = hidden.astype(F32)
        scale = lax.rsqrt(jnp.mean(hidden * hidden, axis=-1, keepdims=True) + 1e-05)
        normed_ref[...] = (hidden * scale * gain_ref[...]).astype(BF16)

    in_vmem = pl.BlockSpec(memory_space=pltpu.VMEM)
    return pl.pallas_call(
        body,
        out_shape=(jax.ShapeDtypeStruct((rows, width), BF16),) * 2,
        in_specs=[pl.BlockSpec(memory_space=pltpu.SMEM)] + [in_vmem] * (NX + 1),
        out_specs=(in_vmem,) * 2,
        scratch_shapes=[pltpu.VMEM((rows, NX * QUARTER), BF16)],
        compiler_params=pltpu.CompilerParams(vmem_limit_bytes=16 << 20),
    )(x.reshape(1), gain.reshape(1, -1), *quarters)


def ranks_of(expert_ids):
    rows = expert_ids.shape[0]
    experts = jnp.arange(NZ * NY * NC, dtype=jnp.int32)
    named = expert_ids[:, :, None] == experts
    marks = jnp.sum(named.astype(F32), axis=1).astype(BF16)
    steps = jnp.arange(rows)
    earlier = (steps[:, None] > steps[None, :]).astype(BF16)
    counts = jnp.dot(earlier, marks, preferred_element_type=F32)
    return jnp.sum(jnp.where(named, counts[:, None, :], 0.0), axis=2)


def call(body, outs, args, scratch=(), flops=0, limit=16, scalars=0):
    moved_bytes = sum(a.size * a.dtype.itemsize for a in (*args, *outs))
    return pl.pallas_call(
        body,
        out_shape=tuple(outs),
        in_specs=[pl.BlockSpec(memory_space=pltpu.SMEM)] * scalars
        + [pl.BlockSpec(memory_space=pltpu.VMEM)] * (len(args) - scalars),
        out_specs=tuple(pl.BlockSpec(memory_space=pltpu.VMEM) for _ in outs),
        scratch_shapes=list(scratch),
        compiler_params=pltpu.CompilerParams(vmem_limit_bytes=limit << 20),
        cost_estimate=pl.CostEstimate(
            flops=flops, bytes_accessed=moved_bytes, transcendentals=0
        ),
    )(*args)


def pick_rows(spots, base, blocks, joined=False):
    pieces = [b if isinstance(b, tuple) else (b,) for b in blocks]
    flat = [piece for b in pieces for piece in b]
    count, (rows, width) = len(blocks), blocks[0].shape

    def body(spots_ref, *refs):
        ins, outs, whole = refs[: len(flat)], refs[len(flat) : -1], refs[-1]
        slot = lax.broadcasted_iota(jnp.int32, (SLOTS, rows), 0)
        at = 0
        for b in range(count):
            if len(pieces[b]) > 1:
                first = 0
                for piece in pieces[b]:
                    whole[first : first + piece.shape[0], :] = ins[at][...]
                    first, at = first + piece.shape[0], at + 1
                block = whole[...]
            else:
                block, at = ins[at][...], at + 1
            pick = jnp.zeros((SLOTS, rows), F32)
            for r in range(TOP):
                pick += jnp.where(spots_ref[base + b, r : r + 1, :] == slot, 1.0, 0.0)
            found = jnp.dot(pick.astype(BF16), block, preferred_element_type=F32).astype(BF16)
            for i in range(len(WAYS)):
                to, first = (outs[0], i * count * CAP) if joined else (outs[i], 0)
                first += b * CAP
                to[first : first + CAP, :] = found[i * CAP : (i + 1) * CAP]

    outs = [jax.ShapeDtypeStruct((count * CAP, width), BF16)] * len(WAYS)
    if joined:
        outs = [jax.ShapeDtypeStruct((len(WAYS) * count * CAP, width), BF16)]
    flops = 2 * count * SLOTS * rows * width
    return call(body, outs, [spots, *flat], [pltpu.VMEM((rows, width), BF16)], flops)


def run_expert(parts, gate_up, down):
    rows, width = parts[0].shape
    total, units = rows * len(parts), down.shape[0]
    wide, tall = 512, 128

    def body(gate_up_ref, down_ref, *refs):
        ins, outs = refs[: len(parts)], refs[len(parts) : -2]
        taken, projected = refs[-2:]
        for i, part in enumerate(ins):
            taken[i * rows : (i + 1) * rows, :] = part[...]
        for first in range(0, 2 * units, wide):
            last = min(first + wide, 2 * units)
            projected[:, first:last] = jnp.dot(
                taken[...], gate_up_ref[:, first:last], preferred_element_type=F32
            )
        for first in range(0, total, tall):
            gate = projected[first : first + tall, :units]
            up = projected[first : first + tall, units:]
            active = (up + 1.0) * gate * jax.nn.sigmoid(1.702 * gate)
            taken[first : first + tall, :] = active.astype(BF16)
        for first in range(0, width, wide):
            last = min(first + wide, width)
            made = jnp.dot(taken[...], down_ref[:, first:last], preferred_element_type=F32)
            made = made.astype(BF16)
            for i, out in enumerate(outs):
                out[:, first:last] = made[i * rows : (i + 1) * rows]

    outs = [jax.ShapeDtypeStruct((rows, width), BF16)] * len(parts)
    scratch = [pltpu.VMEM((total, width), BF16), pltpu.VMEM((total, 2 * units), F32)]
    flops = 6 * total * width * units
    return call(body, outs, [gate_up, down, *parts], scratch, flops, limit=32)


def combine(spots, shares, base, parts, count):
    width = parts[0].shape[1]
    rows = spots.shape[2]

    def body(spots_ref, shares_ref, *refs):
        ins, outs, whole = refs[: len(parts)], refs[len(parts) : -1], refs[-1]
        slot = lax.broadcasted_iota(jnp.int32, (SLOTS, rows), 0)
        for b in range(count):
            for i in range(len(WAYS)):
                part, first = (ins[i], 0) if len(parts) > 1 else (ins[0], i * count * CAP)
                first += b * CAP
                whole[i * CAP : (i + 1) * CAP, :] = part[first : first + CAP, :]
            sums = 0.0
            for fine in range(2):
                share = jnp.zeros((SLOTS, rows), F32)
                for r in range(TOP):
                    here = spots_ref[base + b, r : r + 1, :] == slot
                    at = fine * TOP + r
                    share += jnp.where(here, shares_ref[base + b, at : at + 1, :], 0.0)
                sums += jnp.dot(share.T.astype(BF16), whole[...], preferred_element_type=F32)
            outs[b][...] = sums

    outs = [jax.ShapeDtypeStruct((rows, width), F32)] * count
    flops = 4 * count * SLOTS * rows * width
    return call(body, outs, [spots, shares, *parts], [pltpu.VMEM((SLOTS, width), BF16)], flops)


def shards(
    query_heads,
    key_heads,
    value_heads,
    out_weight,
    norm_gain,
    gate_up_weight,
    down_weight,
    expert_ids,
    route_weights,
):
    tok_rows = query_heads.shape[0]
    device_index = lax.axis_index("ep")
    z, y, c = device_index // (NY * NC), device_index // NC % NY, device_index % NC
    first_pos = device_index * tok_rows

    def plan_of(ids, weights):
        coarse = lax.reduce_precision(weights, 8, 7)
        fine = lax.reduce_precision(weights - coarse, 8, 7)
        lanes = [
            jnp.concatenate([ids.astype(F32).T, ranks_of(ids).T], 0),
            jnp.concatenate([coarse.T, fine.T], 0),
        ]
        plan = jnp.concatenate([*lanes, jnp.zeros_like(lanes[0])], 1).astype(BF16)
        return jnp.concatenate([plan, jnp.zeros_like(plan)], 0)

    def before_of(keys, values):
        return from_behind((keys, values), 1), (keys, values)

    def attend(queries, before, here):
        return window_attention(queries, before, here, first_pos)

    x = lax.axis_index("dp")
    quarters, spots, shares = projection(
        (attend, query_heads),
        (before_of, (key_heads, value_heads)),
        (plan_of, (expert_ids, route_weights)),
        out_weight,
        x,
        z,
        y,
        c,
    )
    hidden, normed = join_and_norm(quarters, norm_gain, x)

    near_count, half = len(GROUPS[0]), tok_rows // 2
    every = range(len(WAYS))

    def spread(rows, lots, back=False):
        sign = -1 if back else 1
        return {i: moved(rows[i], dy=sign * WAYS[i][0], flip=WAYS[i][1]) for i in lots}

    same_plane = [[index_of(i, j, k) for j in range(NY) for k in range(NC)] for i in range(NZ)]

    def exchange(rows):
        rows = rows.reshape(NY * NC, -1, rows.shape[1])
        rows = lax.all_to_all(
            rows, "ep", split_axis=0, concat_axis=0, tiled=True, axis_index_groups=same_plane
        )
        return rows.reshape(-1, rows.shape[2])

    up, down = moved(normed, dz=1), moved(normed, dz=-1)
    held = [normed, down, up]
    up, down = moved(up, dz=1), moved(down, dz=-1)
    [rows] = pick_rows(spots, 0, [*held, down, up], joined=True)
    up, down, rows = tied((up, down, rows))
    got = exchange(rows)
    up, down = moved(up, dz=1), moved(down, dz=-1)
    held = [down, up]
    low, high = moved(up[:half], dz=1), moved(down[half:], dz=-1)
    far_rows = pick_rows(spots, near_count, [*held, (low, high)])
    far_got = spread(far_rows, every)
    [made] = run_expert([got], gate_up_weight[0], down_weight[0])
    far_got, made = tied((far_got, made))
    far_made = run_expert([far_got[i] for i in every], gate_up_weight[0], down_weight[0])
    far_back = spread(far_made, every, back=True)
    sums = combine(spots, shares, near_count, [far_back[i] for i in every], len(GROUPS[1]))
    partial = dict(zip(GROUPS[1], sums))
    back = exchange(made)
    up = moved(partial[4][half:].astype(BF16), dz=1)
    down = moved(partial[4][:half].astype(BF16), dz=-1)
    up = partial[3] + jnp.pad(up.astype(F32), ((half, 0), (0, 0)))
    down = partial[-3] + jnp.pad(down.astype(F32), ((0, half), (0, 0)))
    up, down = moved(up.astype(BF16), dz=1), moved(down.astype(BF16), dz=-1)
    sums = combine(spots, shares, 0, [back], near_count)
    partial.update(zip(GROUPS[0], sums))
    up, down = up.astype(F32) + partial[2], down.astype(F32) + partial[-2]
    for step in (1, 0):
        up = moved(up.astype(BF16), dz=1).astype(F32)
        down = moved(down.astype(BF16), dz=-1).astype(F32)
        if step:
            up, down = up + partial[step], down + partial[-step]
    return (hidden.astype(F32) + (partial[0] + up + down)).astype(BF16)


def solution(mesh):
    placed = (
        P(("dp", "ep"), None),
        P(("dp", "ep"), None),
        P(("dp", "ep"), None),
        P("ep", None),
        P(),
        P("ep", None, None),
        P("ep", None, None),
        P(("dp", "ep"), None),
        P(("dp", "ep"), None),
    )
    return jax.shard_map(
        shards, mesh=mesh, in_specs=placed, out_specs=P(("dp", "ep"), None), check_vma=False
    )
```

```python
import jax
import jax.numpy as jnp
from jax import lax
from jax.experimental import pallas as pl
from jax.experimental.pallas import tpu as pltpu
from jax.sharding import PartitionSpec as P

HD = 64
WIN = 128
NX, NZ, NY, NC = 4, 8, 4, 2
CAP = 16
QUARTER = 384
SLOTS = NY * NC * CAP
GROUPS = ((0, 1, -1, 2, -2), (3, -3, 4))
WAYS = tuple((dy, flip) for dy in range(NY) for flip in range(NC))
TOP = 4
BF16 = jnp.bfloat16
F32 = jnp.float32


def tied(values):
    return lax.optimization_barrier(values)


def index_of(z, y, c):
    return ((z % NZ) * NY + y % NY) * NC + c


def moved(block, dz=0, dy=0, flip=False):
    if not (dz or dy or flip):
        return block
    route = [
        (index_of(z, y, c), index_of(z + dz, y + dy, 1 - c if flip else c))
        for z in range(NZ)
        for y in range(NY)
        for c in range(NC)
    ]
    return lax.ppermute(block, "ep", route)


def from_behind(block, distance):
    devices = range(NZ * NY * NC)
    route = [(i - distance, i) for i in devices if i - distance in devices]
    return lax.ppermute(block, "ep", route)


def window_attention(queries, before, here, first_pos):
    rows, width = queries.shape
    heads_width = here[0].shape[1]
    group = width // heads_width
    lanes = 2 * HD

    def body(first_ref, query_ref, *refs):
        *ins, out_ref, keys, values = refs
        for i, to in enumerate((keys, values)):
            to[:rows, :] = ins[0][:, i * heads_width : (i + 1) * heads_width]
            to[rows:, :] = ins[1 + i][...]
        row = lax.broadcasted_iota(jnp.int32, (rows, 2 * rows), 0)
        key = lax.broadcasted_iota(jnp.int32, (rows, 2 * rows), 1)
        distance = row + rows - key
        allowed = (distance >= 0) & (distance < WIN) & (first_ref[0] - rows + key >= 0)
        half = lax.broadcasted_iota(jnp.int32, (2 * rows, lanes), 1) // HD
        for g in range(heads_width // HD):
            sides = []
            for ref in (keys, values):
                pair = ref[:, g // 2 * lanes : (g // 2 + 1) * lanes].astype(F32)
                alone = jnp.where(half == g % 2, pair, 0.0)
                both = [alone.astype(BF16), pltpu.roll(alone, HD, 1).astype(BF16)]
                sides.append(both if g % 2 == 0 else both[::-1])
            for p in range(group // 2):
                first = g * group * HD + p * lanes
                query = query_ref[:, first : first + lanes]
                mixed = 0.0
                for key_side, value_side in zip(*sides):
                    scores = lax.dot_general(
                        query, key_side, (((1,), (1,)), ((), ())), preferred_element_type=F32
                    ) * HD ** (-0.5)
                    scores = jnp.where(allowed, scores, -1e30)
                    exp_scores = jnp.exp(scores - jnp.max(scores, axis=-1, keepdims=True))
                    whole = jnp.sum(exp_scores, axis=-1, keepdims=True)
                    probs = (exp_scores * (1.0 / whole)).astype(BF16)
                    mixed += jnp.dot(probs, value_side, preferred_element_type=F32)
                out_ref[:, first : first + lanes] = mixed.astype(BF16)

    outs = [jax.ShapeDtypeStruct((rows, width), BF16)]
    scratch = [pltpu.VMEM((2 * rows, heads_width), BF16)] * 2
    args = [first_pos.reshape(1), queries, before, *here]
    return call(body, outs, args, scratch, 80 * rows * rows * width, scalars=1)[0]


def moved_x(block, dx):
    return lax.ppermute(block, "dp", [(x, (x + dx) % NX) for x in range(NX)])


def in_order(pieces, first, count):
    return lax.dynamic_slice_in_dim(jnp.stack(pieces + pieces), (count - first) % count, count, 0)


def projection(attend, before_of, plan_of, out_weight, x, z, y, c):
    depth, width = out_weight.shape
    padded = jnp.pad(out_weight, ((0, 0), (0, NX * QUARTER - width)))
    kept = lax.dynamic_slice_in_dim(padded, x * QUARTER, QUARTER, 1)
    (attend, queries), (before_of, before), (plan_of, plan) = attend, before_of, plan_of
    swapped, before, plan = tied((moved(kept, flip=True), before, plan))
    plan, span = plan_of(*plan), before_of(*before)
    chip = in_order([kept, swapped], c, NC).reshape(-1, QUARTER)
    around = [chip, moved(chip, dy=-1), moved(chip, dy=2), moved(chip, dy=1)]
    plane = in_order(around, y, NY).reshape(-1, QUARTER)
    taken = plane.shape[0]
    plane, queries = tied((jnp.concatenate([plane, plan], 0), queries))
    split = plane.shape[0] // 2 // 16 * 16
    up, down, context = tied(
        (moved(plane, dz=1), moved(plane, dz=-1), attend(queries, *span))
    )
    parts = {0: plane, -1: up, 1: down}
    for step in (2, 3):
        up, down = moved(up, dz=1), moved(down, dz=-1)
        parts[-step], parts[step] = up, down
    parts[4] = (moved(up[:split], dz=1), moved(down[split:], dz=-1))
    rows = context.shape[0]
    up, down = moved_x(context, 1), moved_x(context, -1)
    low, high = moved_x(up[: rows // 2], 1), moved_x(down[rows // 2 :], -1)
    *quarters, spots, shares = multiply(parts, [context, down, low, high, up], (z, y, c))
    quarters = [
        quarters[0],
        moved_x(quarters[3], -1),
        moved_x(quarters[2], 2),
        moved_x(quarters[1], 1),
    ]
    return quarters, spots, shares


def multiply(parts, contexts, place):
    order = [d for group in GROUPS for d in group]
    pieces = [parts[d] if isinstance(parts[d], tuple) else (parts[d],) for d in order]
    flat = [piece for b in pieces for piece in b]
    taken, depth = parts[0].shape[0], contexts[0].shape[1]
    share = depth // NZ
    rows = contexts[0].shape[0]
    tall = sum(b.shape[0] for b in contexts)

    def body(place_ref, *refs):
        weights, ins = refs[: len(flat)], refs[len(flat) : len(flat) + len(contexts)]
        *outs, spots_ref, shares_ref, whole, joined = refs[len(flat) + len(contexts) :]
        z, y, c = place_ref[0], place_ref[1], place_ref[2]
        first = 0
        for piece in ins:
            whole[first : first + piece.shape[0], :] = piece[...]
            first += piece.shape[0]
        total = jnp.zeros((tall, QUARTER), F32)
        at = 0
        for k, d in enumerate(order):
            part = weights[at]
            if len(pieces[k]) > 1:
                first = 0
                for piece in pieces[k]:
                    joined[first : first + piece.shape[0], :] = weights[at][...]
                    first, at = first + piece.shape[0], at + 1
                part = joined
            else:
                at += 1
            column = pl.multiple_of(lax.rem(z + (d + NZ), NZ) * share, share)
            total += jnp.dot(
                whole[:, pl.ds(column, share)], part[:share, :], preferred_element_type=F32
            )
            plan = part[share : share + 2 * TOP, :].astype(F32)
            expert = plan[:TOP, :rows].astype(jnp.int32) - z * (NY * NC)
            rank = plan[TOP:, :rows].astype(jnp.int32)
            way = expert
            if k >= len(GROUPS[0]):
                way = (((expert >> 1) - y) & (NY - 1)) * NC + ((expert & 1) ^ c)
            here = (expert >= 0) & (expert < NY * NC)
            spots_ref[k] = jnp.where(here, way * CAP + rank, -1)
            shares_ref[k] = plan[:, rows : 2 * rows]
        total = total.astype(BF16)
        for k, out in enumerate(outs):
            out[...] = total[k * rows : (k + 1) * rows]

    outs = [jax.ShapeDtypeStruct((rows, QUARTER), BF16)] * NX
    outs.append(jax.ShapeDtypeStruct((NZ, TOP, rows), jnp.int32))
    outs.append(jax.ShapeDtypeStruct((NZ, 2 * TOP, rows), F32))
    scratch = [pltpu.VMEM((tall, depth), BF16), pltpu.VMEM((taken, QUARTER), BF16)]
    args = [jnp.stack(place), *flat, *contexts]
    return call(body, outs, args, scratch, 2 * tall * depth * QUARTER, scalars=1)


def join_and_norm(quarters, gain, x):
    rows, width = quarters[0].shape[0], gain.shape[0]

    def body(x_ref, gain_ref, *refs):
        ins, (hidden_ref, normed_ref, whole) = refs[:NX], refs[NX:]
        for k, piece in enumerate(ins):
            first = pl.multiple_of((x_ref[0] + k) % NX * QUARTER, QUARTER)
            whole[:, pl.ds(first, QUARTER)] = piece[...]
        hidden = whole[:, :width]
        hidden_ref[...] = hidden
        hidden = hidden.astype(F32)
        scale = lax.rsqrt(jnp.mean(hidden * hidden, axis=-1, keepdims=True) + 1e-05)
        normed_ref[...] = (hidden * scale * gain_ref[...]).astype(BF16)

    in_vmem = pl.BlockSpec(memory_space=pltpu.VMEM)
    return pl.pallas_call(
        body,
        out_shape=(jax.ShapeDtypeStruct((rows, width), BF16),) * 2,
        in_specs=[pl.BlockSpec(memory_space=pltpu.SMEM)] + [in_vmem] * (NX + 1),
        out_specs=(in_vmem,) * 2,
        scratch_shapes=[pltpu.VMEM((rows, NX * QUARTER), BF16)],
        compiler_params=pltpu.CompilerParams(vmem_limit_bytes=16 << 20),
    )(x.reshape(1), gain.reshape(1, -1), *quarters)


def ranks_of(expert_ids):
    rows = expert_ids.shape[0]
    experts = jnp.arange(NZ * NY * NC, dtype=jnp.int32)
    named = expert_ids[:, :, None] == experts
    marks = jnp.sum(named.astype(F32), axis=1).astype(BF16)
    steps = jnp.arange(rows)
    earlier = (steps[:, None] > steps[None, :]).astype(BF16)
    counts = jnp.dot(earlier, marks, preferred_element_type=F32)
    return jnp.sum(jnp.where(named, counts[:, None, :], 0.0), axis=2)


def call(body, outs, args, scratch=(), flops=0, limit=16, scalars=0):
    moved_bytes = sum(a.size * a.dtype.itemsize for a in (*args, *outs))
    return pl.pallas_call(
        body,
        out_shape=tuple(outs),
        in_specs=[pl.BlockSpec(memory_space=pltpu.SMEM)] * scalars
        + [pl.BlockSpec(memory_space=pltpu.VMEM)] * (len(args) - scalars),
        out_specs=tuple(pl.BlockSpec(memory_space=pltpu.VMEM) for _ in outs),
        scratch_shapes=list(scratch),
        compiler_params=pltpu.CompilerParams(vmem_limit_bytes=limit << 20),
        cost_estimate=pl.CostEstimate(
            flops=flops, bytes_accessed=moved_bytes, transcendentals=0
        ),
    )(*args)


def pick_rows(spots, base, blocks, joined=False):
    pieces = [b if isinstance(b, tuple) else (b,) for b in blocks]
    flat = [piece for b in pieces for piece in b]
    count, (rows, width) = len(blocks), blocks[0].shape

    def body(spots_ref, *refs):
        ins, outs, whole = refs[: len(flat)], refs[len(flat) : -1], refs[-1]
        slot = lax.broadcasted_iota(jnp.int32, (SLOTS, rows), 0)
        at = 0
        for b in range(count):
            if len(pieces[b]) > 1:
                first = 0
                for piece in pieces[b]:
                    whole[first : first + piece.shape[0], :] = ins[at][...]
                    first, at = first + piece.shape[0], at + 1
                block = whole[...]
            else:
                block, at = ins[at][...], at + 1
            pick = jnp.zeros((SLOTS, rows), F32)
            for r in range(TOP):
                pick += jnp.where(spots_ref[base + b, r : r + 1, :] == slot, 1.0, 0.0)
            found = jnp.dot(pick.astype(BF16), block, preferred_element_type=F32).astype(BF16)
            for i in range(len(WAYS)):
                to, first = (outs[0], i * count * CAP) if joined else (outs[i], 0)
                first += b * CAP
                to[first : first + CAP, :] = found[i * CAP : (i + 1) * CAP]

    outs = [jax.ShapeDtypeStruct((count * CAP, width), BF16)] * len(WAYS)
    if joined:
        outs = [jax.ShapeDtypeStruct((len(WAYS) * count * CAP, width), BF16)]
    flops = 2 * count * SLOTS * rows * width
    return call(body, outs, [spots, *flat], [pltpu.VMEM((rows, width), BF16)], flops)


def run_expert(parts, gate_up, down):
    rows, width = parts[0].shape
    total, units = rows * len(parts), down.shape[0]
    wide, tall = 512, 128

    def body(gate_up_ref, down_ref, *refs):
        ins, outs = refs[: len(parts)], refs[len(parts) : -2]
        taken, projected = refs[-2:]
        for i, part in enumerate(ins):
            taken[i * rows : (i + 1) * rows, :] = part[...]
        for first in range(0, 2 * units, wide):
            last = min(first + wide, 2 * units)
            projected[:, first:last] = jnp.dot(
                taken[...], gate_up_ref[:, first:last], preferred_element_type=F32
            )
        for first in range(0, total, tall):
            gate = projected[first : first + tall, :units]
            up = projected[first : first + tall, units:]
            active = (up + 1.0) * gate * jax.nn.sigmoid(1.702 * gate)
            taken[first : first + tall, :] = active.astype(BF16)
        for first in range(0, width, wide):
            last = min(first + wide, width)
            made = jnp.dot(taken[...], down_ref[:, first:last], preferred_element_type=F32)
            made = made.astype(BF16)
            for i, out in enumerate(outs):
                out[:, first:last] = made[i * rows : (i + 1) * rows]

    outs = [jax.ShapeDtypeStruct((rows, width), BF16)] * len(parts)
    scratch = [pltpu.VMEM((total, width), BF16), pltpu.VMEM((total, 2 * units), F32)]
    flops = 6 * total * width * units
    return call(body, outs, [gate_up, down, *parts], scratch, flops, limit=32)


def combine(spots, shares, base, parts, count):
    width = parts[0].shape[1]
    rows = spots.shape[2]

    def body(spots_ref, shares_ref, *refs):
        ins, outs, whole = refs[: len(parts)], refs[len(parts) : -1], refs[-1]
        slot = lax.broadcasted_iota(jnp.int32, (SLOTS, rows), 0)
        for b in range(count):
            for i in range(len(WAYS)):
                part, first = (ins[i], 0) if len(parts) > 1 else (ins[0], i * count * CAP)
                first += b * CAP
                whole[i * CAP : (i + 1) * CAP, :] = part[first : first + CAP, :]
            sums = 0.0
            for fine in range(2):
                share = jnp.zeros((SLOTS, rows), F32)
                for r in range(TOP):
                    here = spots_ref[base + b, r : r + 1, :] == slot
                    at = fine * TOP + r
                    share += jnp.where(here, shares_ref[base + b, at : at + 1, :], 0.0)
                sums += jnp.dot(share.T.astype(BF16), whole[...], preferred_element_type=F32)
            outs[b][...] = sums

    outs = [jax.ShapeDtypeStruct((rows, width), F32)] * count
    flops = 4 * count * SLOTS * rows * width
    return call(body, outs, [spots, shares, *parts], [pltpu.VMEM((SLOTS, width), BF16)], flops)


def shards(
    query_heads,
    key_heads,
    value_heads,
    out_weight,
    norm_gain,
    gate_up_weight,
    down_weight,
    expert_ids,
    route_weights,
):
    tok_rows = query_heads.shape[0]
    device_index = lax.axis_index("ep")
    z, y, c = device_index // (NY * NC), device_index // NC % NY, device_index % NC
    first_pos = device_index * tok_rows

    def plan_of(ids, weights):
        coarse = lax.reduce_precision(weights, 8, 7)
        fine = lax.reduce_precision(weights - coarse, 8, 7)
        lanes = [
            jnp.concatenate([ids.astype(F32).T, ranks_of(ids).T], 0),
            jnp.concatenate([coarse.T, fine.T], 0),
        ]
        plan = jnp.concatenate([*lanes, jnp.zeros_like(lanes[0])], 1).astype(BF16)
        return jnp.concatenate([plan, jnp.zeros_like(plan)], 0)

    def before_of(keys, values):
        return from_behind(jnp.concatenate([keys, values], 1), 1), (keys, values)

    def attend(queries, before, here):
        return window_attention(queries, before, here, first_pos)

    x = lax.axis_index("dp")
    quarters, spots, shares = projection(
        (attend, query_heads),
        (before_of, (key_heads, value_heads)),
        (plan_of, (expert_ids, route_weights)),
        out_weight,
        x,
        z,
        y,
        c,
    )
    hidden, normed = join_and_norm(quarters, norm_gain, x)

    near_count, half = len(GROUPS[0]), tok_rows // 2
    every = range(len(WAYS))

    def spread(rows, lots, back=False):
        sign = -1 if back else 1
        return {i: moved(rows[i], dy=sign * WAYS[i][0], flip=WAYS[i][1]) for i in lots}

    same_plane = [[index_of(i, j, k) for j in range(NY) for k in range(NC)] for i in range(NZ)]

    def exchange(rows):
        rows = rows.reshape(NY * NC, -1, rows.shape[1])
        rows = lax.all_to_all(
            rows, "ep", split_axis=0, concat_axis=0, tiled=True, axis_index_groups=same_plane
        )
        return rows.reshape(-1, rows.shape[2])

    up, down = moved(normed, dz=1), moved(normed, dz=-1)
    held = [normed, down, up]
    up, down = moved(up, dz=1), moved(down, dz=-1)
    [rows] = pick_rows(spots, 0, [*held, down, up], joined=True)
    up, down, rows = tied((up, down, rows))
    got = exchange(rows)
    up, down = moved(up, dz=1), moved(down, dz=-1)
    held = [down, up]
    low, high = moved(up[:half], dz=1), moved(down[half:], dz=-1)
    far_rows = pick_rows(spots, near_count, [*held, (low, high)])
    far_got = spread(far_rows, every)
    [made] = run_expert([got], gate_up_weight[0], down_weight[0])
    far_got, made = tied((far_got, made))
    far_made = run_expert([far_got[i] for i in every], gate_up_weight[0], down_weight[0])
    far_back = spread(far_made, every, back=True)
    sums = combine(spots, shares, near_count, [far_back[i] for i in every], len(GROUPS[1]))
    partial = dict(zip(GROUPS[1], sums))
    back = exchange(made)
    up = moved(partial[4][half:].astype(BF16), dz=1)
    down = moved(partial[4][:half].astype(BF16), dz=-1)
    up = partial[3] + jnp.pad(up.astype(F32), ((half, 0), (0, 0)))
    down = partial[-3] + jnp.pad(down.astype(F32), ((0, half), (0, 0)))
    up, down = moved(up.astype(BF16), dz=1), moved(down.astype(BF16), dz=-1)
    sums = combine(spots, shares, 0, [back], near_count)
    partial.update(zip(GROUPS[0], sums))
    up, down = up.astype(F32) + partial[2], down.astype(F32) + partial[-2]
    for step in (1, 0):
        up = moved(up.astype(BF16), dz=1).astype(F32)
        down = moved(down.astype(BF16), dz=-1).astype(F32)
        if step:
            up, down = up + partial[step], down + partial[-step]
    return (hidden.astype(F32) + (partial[0] + up + down)).astype(BF16)


def solution(mesh):
    placed = (
        P(("dp", "ep"), None),
        P(("dp", "ep"), None),
        P(("dp", "ep"), None),
        P("ep", None),
        P(),
        P("ep", None, None),
        P("ep", None, None),
        P(("dp", "ep"), None),
        P(("dp", "ep"), None),
    )
    return jax.shard_map(
        shards, mesh=mesh, in_specs=placed, out_specs=P(("dp", "ep"), None), check_vma=False
    )
```
